32 devices in a mesh: strip: 4 (over y, core), depth: 8 (over z, x).
Axes of the slice: x: 2, y: 2, z: 4, core: 2. Of those that a mesh axis runs over, the one named last changes fastest.
Arguments:
- position: float32 [4, 8, 3, 32, 128], P('strip', 'depth'), may hold values from -2.4 to 2.4
- velocity: float32 [4, 8, 3, 32, 128], P('strip', 'depth'), may hold values from -3 to 3
- stress: float32 [4, 8, 6, 32, 128], P('strip', 'depth'), may hold values from -6 to 6
- plastic: float32 [4, 8, 32, 128], P('strip', 'depth'), may hold values from 0.005 to 0.2
- particle_mass: float32 [4, 8, 32, 128], P('strip', 'depth'), may hold values from 0.004 to 0.016
- density: float32 [4, 8, 32, 128], P('strip', 'depth'), may hold values from 0.6 to 1.6
- cohesion: float32 [4, 8, 32, 128], P('strip', 'depth'), may hold values from 0.3 to 1.2
- counts: int32 [4, 8, 32], P('strip', 'depth'), may hold values from 32 to 128, as said below
- block_pairs: int32 [4, 8, 128, 2], P('strip', 'depth'), may hold values from 0 to 31, as said below
- pair_count: int32 [4, 8], P('strip', 'depth'), may hold values from 32 to 128, as said below
- send_lists: int32 [4, 8, 4, 16], P('strip', 'depth'), may hold values from 0 to 31, as said below
- cross_links: int32 [4, 8, 2, 48, 2], P('strip', 'depth'), may hold values from 0 to 15, as said below
- contact: int32 [4, 8, 16], P('strip', 'depth'), may hold values from 0 to 32, as said below
Outputs:
- new_position: float32 [4, 8, 3, 32, 128], P('strip', 'depth')
- new_velocity: float32 [4, 8, 3, 32, 128], P('strip', 'depth')
- new_stress: float32 [4, 8, 6, 32, 128], P('strip', 'depth')
- new_plastic: float32 [4, 8, 32, 128], P('strip', 'depth')
The draws below stay inside these ranges and needn't reach their ends.
Inputs may be any that keep to these rules, and one draw needn't show every extreme that they name: A block's live particles are its first counts slots; every device has a full block. `pair_count`: at least 32; some device reaches 128. `block_pairs`: the first pair_count entries of a device hold each of its blocks paired with itself once and distinct unordered pairs of different blocks, each at most once, in either order; later entries are to be ignored. `send_lists`: each face lists 16 distinct blocks; faces 0, 1 look to the next and previous device along depth, 2, 3 along strip. `cross_links`: entry (f, q) = (a, b): slot a of the device's list 2f meets slot b of the next device's list 2f + 1; a face's entries are distinct. `contact`: 32 stands for no block; a device's entries are either all 32 or 16 distinct blocks.
All inputs are finite; a program needn't handle non-finite values.
Results may differ from the reference program's by a relative error of at most 0.0003.
Values sent between devices are 32-bit elements; how exact they have to be, the bound alone decides.
A program may use at most 64 MiB of HBM per device.

```python
import math
import jax
import jax.numpy as jnp
import numpy as np
from jax import lax

BLOCKS = 32
PARTICLES = 128
PAIR_RATIO = 3
RIM = 16
CROSS = 48
CONTACT = 16
RETURN_ITERS = 4
N_STRIP = 4
N_DEPTH = 8


def band_distance(key):
    centre = jax.random.randint(jax.random.fold_in(key, 101), (N_STRIP, 1), 0, N_DEPTH)
    depth_index = jnp.arange(N_DEPTH, dtype=jnp.int32)[None, :]
    return jnp.abs(depth_index - centre)


def pair_totals(key):
    distance = band_distance(key)
    band_width = max(N_DEPTH // 8, 1)
    off_most = PAIR_RATIO * BLOCKS
    jitter = jax.random.randint(jax.random.fold_in(key, 102), (N_STRIP, N_DEPTH), 0, off_most // 16 + 1)
    jitter = jnp.where(distance > 0, jitter, 0)
    off_live = off_most - jnp.minimum(distance, band_width) * (2 * off_most // 3) // band_width - jitter
    return (BLOCKS + off_live).astype(jnp.int32)


def draw_pair_count(key, part):
    return pair_totals(key)


def draw_block_pairs(key, part):
    totals = pair_totals(key).reshape(-1)
    upper_np, lower_np = np.triu_indices(BLOCKS, 1)
    upper_rows = jnp.asarray(upper_np, jnp.int32)
    upper_cols = jnp.asarray(lower_np, jnp.int32)
    off_most = PAIR_RATIO * BLOCKS
    slot_total = BLOCKS + off_most
    device_keys = jax.random.split(jax.random.fold_in(key, 103), N_STRIP * N_DEPTH)

    def one_device(device_key, live_total):
        pick_key, order_key, swap_key = jax.random.split(device_key, 3)
        chosen = jax.random.permutation(pick_key, upper_np.shape[0])[:off_most]
        diagonal_blocks = jnp.arange(BLOCKS, dtype=jnp.int32)
        row_block = jnp.concatenate([diagonal_blocks, upper_rows[chosen]])
        col_block = jnp.concatenate([diagonal_blocks, upper_cols[chosen]])
        reversed_pair = jax.random.randint(swap_key, (slot_total,), 0, 2)
        row_final = jnp.where(reversed_pair == 1, col_block, row_block)
        col_final = jnp.where(reversed_pair == 1, row_block, col_block)
        slot_index = jnp.arange(slot_total, dtype=jnp.int32)
        ranking = jax.random.permutation(order_key, slot_total).astype(jnp.int32)
        priority = jnp.where(slot_index < live_total, ranking, slot_total + slot_index)
        ordering = jnp.argsort(priority)
        return jnp.stack([row_final[ordering], col_final[ordering]], axis=-1).astype(jnp.int32)
    return jax.vmap(one_device)(device_keys, totals).reshape(N_STRIP, N_DEPTH, slot_total, 2)


def draw_send_lists(key, part):
    face_keys = jax.random.split(jax.random.fold_in(key, 104), N_STRIP * N_DEPTH * 4)

    def one_face(face_key):
        return jax.random.permutation(face_key, BLOCKS)[:RIM].astype(jnp.int32)
    return jax.vmap(one_face)(face_keys).reshape(N_STRIP, N_DEPTH, 4, RIM)


def draw_cross_links(key, part):
    face_keys = jax.random.split(jax.random.fold_in(key, 105), N_STRIP * N_DEPTH * 2)

    def one_face(face_key):
        picked = jax.random.permutation(face_key, RIM * RIM)[:CROSS].astype(jnp.int32)
        return jnp.stack([picked // RIM, picked % RIM], axis=-1)
    return jax.vmap(one_face)(face_keys).reshape(N_STRIP, N_DEPTH, 2, CROSS, 2)


def draw_contact(key, part):
    distance = band_distance(key).reshape(-1)
    device_keys = jax.random.split(jax.random.fold_in(key, 107), N_STRIP * N_DEPTH)

    def one_device(device_key, distance_one):
        picked = jax.random.permutation(device_key, BLOCKS)[:CONTACT].astype(jnp.int32)
        return jnp.where(distance_one <= 1, picked, BLOCKS).astype(jnp.int32)
    return jax.vmap(one_device)(device_keys, distance).reshape(N_STRIP, N_DEPTH, CONTACT)


def draw_counts(key, part):
    fill_key, full_key = jax.random.split(jax.random.fold_in(key, 106))
    counts = jax.random.randint(fill_key, (N_STRIP, N_DEPTH, BLOCKS), 32, PARTICLES + 1)
    full_block = jax.random.randint(full_key, (N_STRIP, N_DEPTH, 1), 0, BLOCKS)
    block_index = jnp.arange(BLOCKS, dtype=jnp.int32)[None, None, :]
    return jnp.where(block_index == full_block, PARTICLES, counts).astype(jnp.int32)


def level_of(key, extent, cuts, low, largest):
    def one(dim, shards_of):
        steps = jax.random.uniform(jax.random.fold_in(jax.random.fold_in(key, 6), dim), (shards_of,), jnp.float32, low / len(cuts), largest / len(cuts))
        return jnp.repeat(jnp.exp(steps), extent[dim] // shards_of).reshape((-1,) + (1,) * (len(extent) - dim - 1))

    loudness = one(*cuts[0])
    for cut in cuts[1:]:
        loudness = loudness * one(*cut)
    return loudness


def bell_draw(key, extent, scale, limit, cuts=(), kind=jnp.bfloat16):
    loudness = level_of(key, extent, cuts, -0.22, 0.18) if cuts else 1.0
    values = jax.random.normal(key, extent, jnp.float32) * scale * loudness
    return jnp.minimum(jnp.maximum(values, -limit), limit).astype(kind)


def setup_inputs(seed: int = 0) -> dict:
    key_of = jax.random.split(jax.random.key(seed), 14)
    position = bell_draw(key_of[0], (N_STRIP, N_DEPTH, 3, BLOCKS, PARTICLES), 0.4, 2.4, ((0, 4), (1, 8)), jnp.float32)
    velocity = bell_draw(key_of[1], (N_STRIP, N_DEPTH, 3, BLOCKS, PARTICLES), 0.5, 3.0, ((0, 4), (1, 8)), jnp.float32)
    stress = bell_draw(key_of[2], (N_STRIP, N_DEPTH, 6, BLOCKS, PARTICLES), 1.0, 6.0, ((0, 4), (1, 8)), jnp.float32)
    plastic = jnp.clip(jnp.exp(math.log(0.2) - 3.6888795 * jax.random.uniform(key_of[3], (N_STRIP, N_DEPTH, BLOCKS, PARTICLES), jnp.float32) ** level_of(key_of[3], (N_STRIP, N_DEPTH, BLOCKS, PARTICLES), ((0, 4), (1, 8)), -0.2, 0.2)), 0.005, 0.2)
    particle_mass = jnp.clip(jnp.exp(math.log(0.016) - 1.3862944 * jax.random.uniform(key_of[4], (N_STRIP, N_DEPTH, BLOCKS, PARTICLES), jnp.float32) ** level_of(key_of[4], (N_STRIP, N_DEPTH, BLOCKS, PARTICLES), ((0, 4), (1, 8)), -0.2, 0.2)), 0.004, 0.016)
    density = jnp.clip(jnp.exp(math.log(1.6) - 0.98082923 * jax.random.uniform(key_of[5], (N_STRIP, N_DEPTH, BLOCKS, PARTICLES), jnp.float32) ** level_of(key_of[5], (N_STRIP, N_DEPTH, BLOCKS, PARTICLES), ((0, 4), (1, 8)), -0.2, 0.2)), 0.6, 1.6)
    cohesion = jnp.clip(jnp.exp(math.log(1.2) - 1.3862944 * jax.random.uniform(key_of[6], (N_STRIP, N_DEPTH, BLOCKS, PARTICLES), jnp.float32) ** level_of(key_of[6], (N_STRIP, N_DEPTH, BLOCKS, PARTICLES), ((0, 4), (1, 8)), -0.2, 0.2)), 0.3, 1.2)
    counts = draw_counts(jax.random.fold_in(key_of[13], 71), 0)
    block_pairs = draw_block_pairs(jax.random.fold_in(key_of[13], 71), 0)
    pair_count = draw_pair_count(jax.random.fold_in(key_of[13], 71), 0)
    send_lists = draw_send_lists(jax.random.fold_in(key_of[13], 71), 0)
    cross_links = draw_cross_links(jax.random.fold_in(key_of[13], 71), 0)
    contact = draw_contact(jax.random.fold_in(key_of[13], 71), 0)
    return dict(position=position, velocity=velocity, stress=stress, plastic=plastic, particle_mass=particle_mass, density=density, cohesion=cohesion, counts=counts, block_pairs=block_pairs, pair_count=pair_count, send_lists=send_lists, cross_links=cross_links, contact=contact)


smooth_len = 1.5
kernel_coef = -105.0 / (3.141592653589793 * 1.5 ** 5)
time_step = 0.25
gravity = 1.0
spin_rate = 2.0
blade_stiff = 4.0
bulk_mod = 2.0
shear_mod = 1.5
friction = 0.25
harden_scale = 0.05
harden_mod = 0.5
relax_rate = 0.7
tau_floor = 0.5
voigt_index = ((0, 3, 5), (3, 1, 4), (5, 4, 2))
voigt_pairs = ((0, 0), (1, 1), (2, 2), (0, 1), (1, 2), (0, 2))

def source_rows(places, motion, stress, particle_mass, density, occupied):
    safe_density = jnp.where(occupied > 0.0, density, 1.0)
    weighted_mass = particle_mass * occupied
    volume = weighted_mass / safe_density
    scaled = stress / (safe_density * safe_density)[..., None, :]
    feature_rows = [weighted_mass]
    for row_axis in range(3):
        feature_rows.append(weighted_mass * places[..., row_axis, :])
    for component in range(6):
        feature_rows.append(weighted_mass * scaled[..., component, :])
    for row_axis in range(3):
        dotted = scaled[..., voigt_index[row_axis][0], :] * places[..., 0, :]
        dotted = dotted + scaled[..., voigt_index[row_axis][1], :] * places[..., 1, :]
        dotted = dotted + scaled[..., voigt_index[row_axis][2], :] * places[..., 2, :]
        feature_rows.append(weighted_mass * dotted)
    feature_rows.append(volume)
    for row_axis in range(3):
        feature_rows.append(volume * motion[..., row_axis, :])
    for row_axis in range(3):
        feature_rows.append(volume * places[..., row_axis, :])
    for row_axis, col_axis in voigt_pairs:
        paired = motion[..., row_axis, :] * places[..., col_axis, :] + motion[..., col_axis, :] * places[..., row_axis, :]
        feature_rows.append(volume * (0.5 * paired))
    return jnp.stack(feature_rows, axis=-2)

def pair_kernel(row_places, col_places, weight):
    squared = jnp.zeros(row_places.shape[:-2] + (row_places.shape[-1], col_places.shape[-1]), jnp.float32)
    for row_axis in range(3):
        spread = row_places[..., row_axis, :, None] - col_places[..., row_axis, None, :]
        squared = squared + spread * spread
    closeness = jnp.maximum(1.0 - jnp.sqrt(squared) / smooth_len, 0.0)
    return kernel_coef * closeness * closeness * closeness * weight[..., None, None]

def tile_terms(row_sources, row_places, col_sources, col_places, weight):
    kernel = pair_kernel(row_places, col_places, weight)
    to_rows = jnp.einsum('tkj,tij->tki', col_sources, kernel, precision=lax.Precision.HIGHEST)
    to_cols = jnp.einsum('tki,tij->tkj', row_sources, kernel, precision=lax.Precision.HIGHEST)
    return (to_rows, to_cols)

def section_rates(summed, places, motion, stress, density, contact_flag):
    scaled = stress / (density * density)[..., None, :]
    blade_motion = (spin_rate * places[..., 2, :], jnp.zeros_like(places[..., 1, :]), -spin_rate * places[..., 0, :])
    acceleration = []
    for row_axis in range(3):
        total_force = jnp.zeros_like(summed[..., 0, :])
        for col_axis in range(3):
            voigt_slot = voigt_index[row_axis][col_axis]
            total_force = total_force + scaled[..., voigt_slot, :] * (places[..., col_axis, :] * summed[..., 0, :] - summed[..., 1 + col_axis, :])
            total_force = total_force + places[..., col_axis, :] * summed[..., 4 + voigt_slot, :]
        total_force = total_force - summed[..., 10 + row_axis, :]
        total_force = total_force + blade_stiff * contact_flag * (blade_motion[row_axis] - motion[..., row_axis, :])
        if row_axis == 2:
            total_force = total_force - gravity
        acceleration.append(total_force)
    strain = []
    for component, (row_axis, col_axis) in enumerate(voigt_pairs):
        strain_rate = 0.5 * (places[..., col_axis, :] * summed[..., 14 + row_axis, :] + places[..., row_axis, :] * summed[..., 14 + col_axis, :])
        strain_rate = strain_rate - summed[..., 20 + component, :]
        strain_rate = strain_rate - 0.5 * summed[..., 13, :] * (motion[..., row_axis, :] * places[..., col_axis, :] + motion[..., col_axis, :] * places[..., row_axis, :])
        strain_rate = strain_rate + 0.5 * (motion[..., row_axis, :] * summed[..., 17 + col_axis, :] + motion[..., col_axis, :] * summed[..., 17 + row_axis, :])
        strain.append(strain_rate)
    return (jnp.stack(acceleration, axis=-2), jnp.stack(strain, axis=-2))

def elastic_step(stress, strain, fraction):
    volumetric = strain[..., 0, :] + strain[..., 1, :] + strain[..., 2, :]
    lame_first = bulk_mod - 2.0 * shear_mod / 3.0
    components = []
    for component in range(6):
        change = 2.0 * shear_mod * strain[..., component, :]
        if component < 3:
            change = change + lame_first * volumetric
        components.append(stress[..., component, :] + fraction * time_step * change)
    return components

def plastic_return(components, plastic, cohesion):
    for iteration in range(RETURN_ITERS):
        mean_stress = (components[0] + components[1] + components[2]) / 3.0
        deviator = [components[0] - mean_stress, components[1] - mean_stress, components[2] - mean_stress, components[3], components[4], components[5]]
        second = 0.5 * (deviator[0] * deviator[0] + deviator[1] * deviator[1] + deviator[2] * deviator[2])
        second = second + deviator[3] * deviator[3] + deviator[4] * deviator[4] + deviator[5] * deviator[5]
        shear_norm = jnp.sqrt(second)
        yield_limit = cohesion * (1.0 + plastic / (plastic + harden_scale))
        excess = jnp.maximum(shear_norm + friction * 3.0 * mean_stress - yield_limit, 0.0)
        multiplier = relax_rate * excess / (shear_mod + 9.0 * bulk_mod * friction * friction + harden_mod)
        shrink = jnp.maximum(1.0 - shear_mod * multiplier / jnp.maximum(shear_norm, tau_floor), 0.0)
        mean_stress = mean_stress - 3.0 * bulk_mod * friction * multiplier
        components = [deviator[0] * shrink + mean_stress, deviator[1] * shrink + mean_stress, deviator[2] * shrink + mean_stress, deviator[3] * shrink, deviator[4] * shrink, deviator[5] * shrink]
        plastic = plastic + multiplier
    return (jnp.stack(components, axis=-2), plastic)

def device_sums(sources, places, block_pairs, pair_count, send_lists, cross_links, depth_sources, depth_places, strip_sources, strip_places):
    slot_index = jnp.arange(block_pairs.shape[0], dtype=jnp.int32)
    row_block = block_pairs[:, 0]
    col_block = block_pairs[:, 1]
    weight = jnp.where(slot_index < pair_count, jnp.where(row_block == col_block, 0.5, 1.0), 0.0).astype(jnp.float32)
    to_rows, to_cols = tile_terms(sources[row_block], places[row_block], sources[col_block], places[col_block], weight)
    summed = jnp.zeros(sources.shape, jnp.float32).at[row_block].add(to_rows).at[col_block].add(to_cols)
    returned = []
    for face_index, far_sources, far_places in ((0, depth_sources, depth_places), (1, strip_sources, strip_places)):
        own_blocks = send_lists[2 * face_index][cross_links[face_index, :, 0]]
        far_slots = cross_links[face_index, :, 1]
        unit_weight = jnp.ones(far_slots.shape, jnp.float32)
        to_rows, to_cols = tile_terms(sources[own_blocks], places[own_blocks], far_sources[far_slots], far_places[far_slots], unit_weight)
        summed = summed.at[own_blocks].add(to_rows)
        returned.append(jnp.zeros(far_sources.shape, jnp.float32).at[far_slots].add(to_cols))
    return (summed, returned[0], returned[1])

def take_rows(table_in, index_list):
    return table_in[index_list]

def add_rows(table_in, index_list, extra):
    return table_in.at[index_list].add(extra)

def flatten_devices(values_in):
    return values_in.reshape((N_STRIP * N_DEPTH,) + values_in.shape[2:])

def unflatten_devices(values_in):
    return values_in.reshape((N_STRIP, N_DEPTH) + values_in.shape[1:])

def reference(position, velocity, stress, plastic, particle_mass, density, cohesion, counts, block_pairs, pair_count, send_lists, cross_links, contact):
    places = jnp.swapaxes(position, 2, 3)
    motion = jnp.swapaxes(velocity, 2, 3)
    stress_blocks = jnp.swapaxes(stress, 2, 3)
    occupied = (jnp.arange(PARTICLES, dtype=jnp.int32)[None, None, None, :] < counts[..., None]).astype(jnp.float32)
    contact_flag = lax.optimization_barrier(jnp.sum((contact[..., :, None] == jnp.arange(BLOCKS, dtype=jnp.int32)).astype(jnp.float32), axis=-2))[..., None]
    take_rim = jax.vmap(jax.vmap(take_rows))
    add_rim = jax.vmap(jax.vmap(add_rows))
    depth_keep = (jnp.arange(N_DEPTH) < N_DEPTH - 1).astype(jnp.float32)[None, :, None, None, None]
    depth_first = (jnp.arange(N_DEPTH) > 0).astype(jnp.float32)[None, :, None, None, None]

    def interact(cur_places, cur_motion, cur_stress):
        sources = source_rows(cur_places, cur_motion, cur_stress, particle_mass, density, occupied)
        depth_sources = jnp.roll(take_rim(sources, send_lists[:, :, 1]), -1, axis=1) * depth_keep
        depth_places = jnp.roll(take_rim(cur_places, send_lists[:, :, 1]), -1, axis=1) * depth_keep
        strip_sources = jnp.roll(take_rim(sources, send_lists[:, :, 3]), -1, axis=0)
        strip_places = jnp.roll(take_rim(cur_places, send_lists[:, :, 3]), -1, axis=0)

        def device_step(device_items):
            return device_sums(*device_items)
        gathered = tuple((flatten_devices(values_in) for values_in in (sources, cur_places, block_pairs, pair_count, send_lists, cross_links, depth_sources, depth_places, strip_sources, strip_places)))
        summed, back_depth, back_strip = lax.map(device_step, gathered)
        summed = unflatten_devices(summed)
        back_depth = jnp.roll(unflatten_devices(back_depth), 1, axis=1) * depth_first
        back_strip = jnp.roll(unflatten_devices(back_strip), 1, axis=0)
        summed = add_rim(summed, send_lists[:, :, 1], back_depth)
        summed = add_rim(summed, send_lists[:, :, 3], back_strip)
        return summed
    summed = interact(places, motion, stress_blocks)
    acceleration, strain = section_rates(summed, places, motion, stress_blocks, density, contact_flag)
    half_motion = motion + 0.5 * time_step * acceleration
    half_places = places + 0.5 * time_step * motion
    half_stress = plastic_return(elastic_step(stress_blocks, strain, 0.5), plastic, cohesion)[0]
    summed = interact(half_places, half_motion, half_stress)
    acceleration, strain = section_rates(summed, half_places, half_motion, half_stress, density, contact_flag)
    new_motion = motion + time_step * acceleration
    new_places = places + time_step * half_motion
    new_stress, new_plastic = plastic_return(elastic_step(stress_blocks, strain, 1.0), plastic, cohesion)
    particle_keep = occupied[..., None, :]
    return (jnp.swapaxes(new_places * particle_keep, 2, 3), jnp.swapaxes(new_motion * particle_keep, 2, 3), jnp.swapaxes(new_stress * particle_keep, 2, 3), new_plastic * occupied)
```

```python
import functools

import jax
import jax.numpy as jnp
from jax import lax
from jax.experimental import pallas as pl
from jax.experimental.pallas import tpu as pltpu
from jax.sharding import PartitionSpec as P

RETURN_ITERS = 4

smooth_len = 1.5
kernel_coef = -105.0 / (3.141592653589793 * 1.5**5)
time_step = 0.25
gravity = 1.0
spin_rate = 2.0
blade_stiff = 4.0
bulk_mod = 2.0
shear_mod = 1.5
friction = 0.25
harden_scale = 0.05
harden_mod = 0.5
relax_rate = 0.7
tau_floor = 0.5
voigt_index = ((0, 3, 5), (3, 1, 4), (5, 4, 2))
voigt_pairs = ((0, 0), (1, 1), (2, 2), (0, 1), (1, 2), (0, 2))

STATE = 16
SOURCES = 26
ROWS = 32
FEATURES = 32
UNROLL = 16
FACE_UNROLL = 4
PITCH = 36
f32 = jnp.float32
bf16 = jnp.bfloat16


def from_behind(block, axis, distance):
    devices = range(lax.axis_size(axis))
    route = [(i - distance, i) for i in devices if i - distance in devices]
    return lax.ppermute(block, axis, route)


def passed_along(value, axis, steps):
    count = lax.axis_size(axis)
    pairs = [(source, (source + steps) % count) for source in range(count)]
    return lax.ppermute(value, axis, pairs)


def source_rows(x, v, s, mass, volume):
    rows = [mass]
    rows += [mass * x[k] for k in range(3)]
    rows += [mass * s[c] for c in range(6)]
    for k in range(3):
        i = voigt_index[k]
        rows.append(mass * (s[i[0]] * x[0] + s[i[1]] * x[1] + s[i[2]] * x[2]))
    rows.append(volume)
    rows += [volume * v[k] for k in range(3)]
    rows += [volume * x[k] for k in range(3)]
    for a, b in voigt_pairs:
        rows.append(volume * (0.5 * (v[a] * x[b] + v[b] * x[a])))
    return rows


def split3(value):
    high = value.astype(bf16).astype(f32)
    rest = value - high
    mid = rest.astype(bf16).astype(f32)
    low = (rest - mid).astype(bf16).astype(f32)
    return high, mid, low


PRODUCTS = ((0, 0), (0, 1), (1, 0), (1, 1), (0, 2), (2, 0))


def distance_rows(x, row_side, col_side):
    scaled = [x[k] * (1.0 / smooth_len) for k in range(3)]
    parts = [split3(y) for y in scaled]
    norm = split3(scaled[0] * scaled[0] + scaled[1] * scaled[1] + scaled[2] * scaled[2])
    one = jnp.ones_like(x[0])
    zero = jnp.zeros_like(x[0])
    left, right = [], []
    for k in range(3):
        for a, b in PRODUCTS:
            left.append(-2.0 * parts[k][a])
            right.append(parts[k][b])
    left += list(norm) + [one] * 3
    right += [one] * 3 + list(norm)
    fill = FEATURES - len(left)
    return (left + [zero] * fill if row_side else None, right + [zero] * fill if col_side else None)


def put_rows(ref, rows, start, count, stride):
    for k, row in enumerate(rows):
        ref[pl.ds(start * stride + k, count, stride=stride), :] = row


def get_row(ref, k, count, stride):
    return ref[pl.ds(k, count, stride=stride), :]


def close_kernel(left, right):
    squared = lax.dot_general(left, right, (((1,), (0,)), ((), ())), preferred_element_type=f32)
    squared = jnp.maximum(squared, 1e-30)
    near = jnp.maximum(1.0 - squared * lax.rsqrt(squared), 0.0)
    return (near * near * near).astype(bf16)


def fold(result):
    return result[:ROWS] + result[ROWS:]


def spread(sources, kernel):
    return fold(
        lax.dot_general(sources, kernel, (((1,), (0,)), ((), ())), preferred_element_type=f32)
    )


def pipelined(groups, width, prepare, apply, acc):
    for u in range(width):
        prepare(0, u, 0)

    def step(i, carry):
        for half in range(2):
            g = 2 * i + half
            found = []
            for u in range(width):
                found += apply(g, u, half)
                prepare(g + 1, u, 1 - half)
            for at, value in found:
                acc[at] += value
        return carry

    lax.fori_loop(0, (groups + 1) // 2, step, 0)


def store_sources(tmp, src, start, count):
    def one(b, carry):
        rows = tmp[pl.ds(b * PITCH, ROWS), :]
        high = rows.astype(bf16)
        src[start + b, 0:ROWS, :] = high
        src[start + b, ROWS : 2 * ROWS, :] = (rows - high.astype(f32)).astype(bf16)
        return carry

    lax.fori_loop(0, count, one, 0, unroll=4)


def store_cols(tmp, col, start, count):
    def one(b, carry):
        col[start + b] = tmp[pl.ds(b * PITCH, FEATURES), :].astype(bf16)
        return carry

    lax.fori_loop(0, count, one, 0, unroll=4)


def store_lefts(tmp, left, start, count):
    def one(b, carry):
        left[start + b] = tmp[pl.ds(b * PITCH, FEATURES), :].T.astype(bf16)
        return carry

    lax.fori_loop(0, count, one, 0, unroll=4)


def gather_rims(rows, raw, lists, sends, blocks):
    put_rows(raw, rows, 0, blocks, STATE)
    for face in range(4):
        for slot in range(lists.shape[1]):
            at = pl.multiple_of(lists[face, slot] * STATE, STATE)
            sends[face][slot * STATE : (slot + 1) * STATE, :] = raw[pl.ds(at, STATE), :]


def begin_kernel(
    counts, lists, links, pos_in, vel_in, stress_in, mass_in, density_in, state, s0, s1, s2, s3,
    occ, raw, pos, vel, stress, mass, density, sems,
):
    moved = ((pos_in, pos), (vel_in, vel), (stress_in, stress), (mass_in, mass), (density_in, density))
    copies = [pltpu.make_async_copy(a, b, sems.at[i]) for i, (a, b) in enumerate(moved)]
    for copy in copies:
        copy.start()
    blocks, parts = mass.shape
    lane = lax.broadcasted_iota(jnp.int32, (1, parts), 1)
    for b in range(blocks):
        occ[b : b + 1, :] = jnp.where(lane < counts[b], 1.0, 0.0)
    live = occ[...]
    for copy in copies:
        copy.wait()
    rho = density[...]
    inverse = 1.0 / (rho * rho)
    weighted = mass[...] * live * kernel_coef
    rows = [pos[k] for k in range(3)] + [vel[k] for k in range(3)]
    rows += [stress[c] * inverse for c in range(6)]
    rows += [weighted, weighted / rho, live, inverse]
    for k, row in enumerate(rows):
        state[k] = row
    gather_rims(rows, raw, lists, (s0, s1, s2, s3), blocks)
    cross = links.shape[2]
    for face, send in ((0, s0), (1, s2)):
        packed = jnp.zeros((1, parts), jnp.int32)
        for side in range(2):
            for q in range(cross):
                packed = jnp.where(lane == side * cross + q, links[face, side, q], packed)
        send[STATE - 1 : STATE, :] = packed.astype(f32)


def local_kernel(pairs, total, state, acc, right, tmp, src, left, held, turned):
    blocks = state.shape[1]
    x = [state[k] for k in range(3)]
    v = [state[k] for k in range(3, 6)]
    s = [state[k] for k in range(6, 12)]
    zero = jnp.zeros_like(x[0])
    rows = source_rows(x, v, s, state[12], state[13])
    put_rows(tmp, rows + [zero] * (ROWS - SOURCES), 0, blocks, PITCH)
    store_sources(tmp, src, 0, blocks)
    left_rows, right_rows = distance_rows(x, True, True)
    put_rows(tmp, right_rows, 0, blocks, PITCH)
    store_cols(tmp, right, 0, blocks)
    put_rows(tmp, left_rows, 0, blocks, PITCH)

    store_lefts(tmp, left, 0, blocks)
    src[blocks] = jnp.zeros(src.shape[1:], bf16)
    right[blocks] = jnp.zeros(right.shape[1:], bf16)
    left[blocks] = jnp.zeros(left.shape[1:], bf16)
    acc[...] = jnp.zeros(acc.shape, f32)
    live = total[0, 0]
    last = pairs.shape[1] - 1

    def entry(q):
        at = jnp.minimum(q, last)
        a, b = pairs[0, at], pairs[1, at]
        return jnp.where(q < live, a, blocks), jnp.where(q < live, b, blocks)

    def prepare(g, u, slot):
        a, b = entry(g * UNROLL + u)
        kernel = close_kernel(left[a], right[b])
        held[slot * UNROLL + u] = kernel
        turned[slot * UNROLL + u] = kernel.T

    def apply(g, u, slot):
        a, b = entry(g * UNROLL + u)
        at = slot * UNROLL + u
        other = jnp.where(a == b, blocks, b)
        return [(a, spread(src[b], turned[at])), (other, spread(src[a], held[at]))]

    pipelined((live + UNROLL - 1) // UNROLL, UNROLL, prepare, apply, acc)


def cross_sums(lists, links, links_behind, far, acc_in, right, acc, tmp, src, left, held):
    rim = lists.shape[1]
    for f in range(4):
        got = [get_row(far[f], k, rim, STATE) for k in range(14)]
        zero = jnp.zeros_like(got[0])
        rows = source_rows(got[0:3], got[3:6], got[6:12], got[12], got[13])
        put_rows(tmp, rows + [zero] * (ROWS - SOURCES), f * rim, rim, PITCH)
    store_sources(tmp, src, 0, 4 * rim)
    for f in range(4):
        got = [get_row(far[f], k, rim, STATE) for k in range(3)]
        put_rows(tmp, distance_rows(got, True, False)[0], f * rim, rim, PITCH)
    store_lefts(tmp, left, 0, 4 * rim)
    left[4 * rim] = jnp.zeros(left.shape[1:], bf16)
    acc[...] = acc_in[...]

    src[4 * rim] = jnp.zeros(src.shape[1:], bf16)
    cross = links.shape[2]
    whole = cross % (2 * FACE_UNROLL) == 0

    def entry(g, u):
        q = g * FACE_UNROLL + u // 4
        at = jnp.minimum(q, cross - 1)
        face, behind = (u % 4) // 2, u % 2
        if behind:
            own = lists[2 * face + 1, links_behind[face][1, at]]
            far_slot = links_behind[face][0, at]
        else:
            own, far_slot = lists[2 * face, links[face, 0, at]], links[face, 1, at]
        far_slot = (u % 4) * rim + far_slot
        return own, far_slot if whole else jnp.where(q < cross, far_slot, 4 * rim)

    width = 4 * FACE_UNROLL

    def prepare(g, u, slot):
        own, far_slot = entry(g, u)
        held[slot * width + u] = close_kernel(left[far_slot], right[own])

    def apply(g, u, slot):
        own, far_slot = entry(g, u)
        return [(own, spread(src[far_slot], held[slot * width + u]))]

    pipelined((cross + FACE_UNROLL - 1) // FACE_UNROLL, width, prepare, apply, acc)


def section_rates(summed, x, v, s, contact_flag):
    blade = (spin_rate * x[2], jnp.zeros_like(x[1]), -spin_rate * x[0])
    acceleration = []
    arm = [x[l] * summed[0] - summed[1 + l] for l in range(3)]
    for k in range(3):
        total = -summed[10 + k] + blade_stiff * contact_flag * (blade[k] - v[k])
        for l in range(3):
            slot = voigt_index[k][l]
            total = total + s[slot] * arm[l] + x[l] * summed[4 + slot]
        if k == 2:
            total = total - gravity
        acceleration.append(total)
    strain = []
    for c, (k, l) in enumerate(voigt_pairs):
        rate = 0.5 * (x[l] * summed[14 + k] + x[k] * summed[14 + l]) - summed[20 + c]
        rate = rate - 0.5 * summed[13] * (v[k] * x[l] + v[l] * x[k])
        rate = rate + 0.5 * (v[k] * summed[17 + l] + v[l] * summed[17 + k])
        strain.append(rate)
    return acceleration, strain


def elastic_step(stress, strain, fraction):
    volumetric = strain[0] + strain[1] + strain[2]
    lame_first = bulk_mod - 2.0 * shear_mod / 3.0
    components = []
    for c in range(6):
        change = 2.0 * shear_mod * strain[c]
        if c < 3:
            change = change + lame_first * volumetric
        components.append(stress[c] + fraction * time_step * change)
    return components


def plastic_return(c, plastic, cohesion):
    for _ in range(RETURN_ITERS):
        mean = (c[0] + c[1] + c[2]) / 3.0
        d = [c[0] - mean, c[1] - mean, c[2] - mean, c[3], c[4], c[5]]
        second = 0.5 * (d[0] * d[0] + d[1] * d[1] + d[2] * d[2])
        second = second + d[3] * d[3] + d[4] * d[4] + d[5] * d[5]
        tau = jnp.sqrt(second)
        limit = cohesion * (1.0 + plastic / (plastic + harden_scale))
        excess = jnp.maximum(tau + friction * 3.0 * mean - limit, 0.0)
        multiplier = (
            relax_rate * excess / (shear_mod + 9.0 * bulk_mod * friction * friction + harden_mod)
        )
        shrink = jnp.maximum(1.0 - shear_mod * multiplier / jnp.maximum(tau, tau_floor), 0.0)
        mean = mean - 3.0 * bulk_mod * friction * multiplier
        c = [
            d[0] * shrink + mean,
            d[1] * shrink + mean,
            d[2] * shrink + mean,
            d[3] * shrink,
            d[4] * shrink,
            d[5] * shrink,
        ]
        plastic = plastic + multiplier
    return c, plastic


def contact_rows(contact, flag, blocks):
    flag[...] = jnp.zeros_like(flag)
    for i in range(contact.shape[0]):
        flag[pl.ds(contact[i], 1), :] += 1.0
    return flag[0:blocks, :]


def rates_of(acc, state, contact, flag):
    blocks, parts = state.shape[1:]
    contact_flag = contact_rows(contact, flag, blocks)
    x = [state[k] for k in range(3)]
    v = [state[k] for k in range(3, 6)]
    s = [state[k] for k in range(6, 12)]
    summed = [acc[0:blocks, k, :] for k in range(SOURCES)]
    return x, v, *section_rates(summed, x, v, s, contact_flag)


def half_kernel(
    lists, links, behind_depth, behind_strip, contact,
    acc_in, right, d_next, d_prev, s_next, s_prev, state, stress, plastic, cohesion,
    state_out, s0, s1, s2, s3,
    acc, tmp, src, left, held, flag, raw,
):
    blocks = state.shape[1]
    cross_sums(
        lists, links, (behind_depth, behind_strip), (d_next, d_prev, s_next, s_prev),
        acc_in, right, acc, tmp, src, left, held,
    )
    x, v, acceleration, strain = rates_of(acc, state, contact, flag)
    components, _ = plastic_return(
        elastic_step([stress[c] for c in range(6)], strain, 0.5), plastic[...], cohesion[...]
    )
    inverse = state[15]
    rows = [x[k] + 0.5 * time_step * v[k] for k in range(3)]
    rows += [v[k] + 0.5 * time_step * acceleration[k] for k in range(3)]
    rows += [c * inverse for c in components]
    rows += [state[12], state[13], state[14], inverse]
    for k, row in enumerate(rows):
        state_out[k] = row
    gather_rims(rows, raw, lists, (s0, s1, s2, s3), blocks)


def end_kernel(
    lists, links, behind_depth, behind_strip, contact,
    acc_in, right, d_next, d_prev, s_next, s_prev, state, stress, plastic, cohesion, position, velocity,
    new_position, new_velocity, new_stress, new_plastic,
    acc, tmp, src, left, held, flag,
):
    cross_sums(
        lists, links, (behind_depth, behind_strip), (d_next, d_prev, s_next, s_prev),
        acc_in, right, acc, tmp, src, left, held,
    )
    _, half_v, acceleration, strain = rates_of(acc, state, contact, flag)
    components, hardened = plastic_return(
        elastic_step([stress[c] for c in range(6)], strain, 1.0), plastic[...], cohesion[...]
    )
    live = state[14]
    for k in range(3):
        new_position[k] = (position[k] + time_step * half_v[k]) * live
        new_velocity[k] = (velocity[k] + time_step * acceleration[k]) * live
    for c in range(6):
        new_stress[c] = components[c] * live
    new_plastic[...] = hardened * live


def shards(
    position, velocity, stress, plastic, particle_mass, density, cohesion,
    counts, block_pairs, pair_count, send_lists, cross_links, contact,
):
    position, velocity, stress = position[0, 0], velocity[0, 0], stress[0, 0]
    plastic, mass, density, cohesion = plastic[0, 0], particle_mass[0, 0], density[0, 0], cohesion[0, 0]
    counts, pairs, lists = counts[0, 0], jnp.swapaxes(block_pairs[0, 0], 0, 1), send_lists[0, 0]
    links, contact = jnp.swapaxes(cross_links[0, 0], 1, 2), contact[0, 0]
    blocks, parts = mass.shape
    rim = lists.shape[1]
    smem = pl.BlockSpec(memory_space=pltpu.SMEM)
    vmem = pl.BlockSpec(memory_space=pltpu.VMEM)
    shape = jax.ShapeDtypeStruct
    state_shape = shape((STATE, blocks, parts), f32)
    send_shape = shape((rim * STATE, parts), f32)
    acc_shape = shape((blocks + 1, ROWS, parts), f32)
    right_shape = shape((blocks + 1, FEATURES, parts), bf16)
    far_scratch = [
        pltpu.VMEM((blocks + 1, ROWS, parts), f32),
        pltpu.VMEM((4 * rim * PITCH, parts), f32),
        pltpu.VMEM((4 * rim + 1, 2 * ROWS, parts), bf16),
        pltpu.VMEM((4 * rim + 1, parts, FEATURES), bf16),
        pltpu.VMEM((8 * FACE_UNROLL, parts, parts), bf16),
        pltpu.VMEM((blocks + 8, parts), f32),
    ]
    raw_scratch = pltpu.VMEM((blocks * STATE, parts), f32)
    params = pltpu.CompilerParams(vmem_limit_bytes=24 << 20)

    cross = links.shape[2]

    def pair_list(rims):
        row = lax.slice(rims, (STATE - 1, 0), (STATE, 2 * cross))
        return row.reshape(2, cross).astype(jnp.int32)

    def exchange(sends):
        return (
            from_behind(sends[1], "depth", -1),
            from_behind(sends[0], "depth", 1),
            passed_along(sends[3], "strip", -1),
            passed_along(sends[2], "strip", 1),
        )

    def local(state):
        tiles = pairs.shape[1]
        return pl.pallas_call(
            local_kernel,
            out_shape=(acc_shape, right_shape),
            in_specs=[smem, smem, vmem],
            out_specs=(vmem, vmem),
            scratch_shapes=[
                pltpu.VMEM((blocks * PITCH, parts), f32),
                pltpu.VMEM((blocks + 1, 2 * ROWS, parts), bf16),
                pltpu.VMEM((blocks + 1, parts, FEATURES), bf16),
                pltpu.VMEM((2 * UNROLL, parts, parts), bf16),
                pltpu.VMEM((2 * UNROLL, parts, parts), bf16),
            ],
            compiler_params=params,
            cost_estimate=pl.CostEstimate(
                flops=tiles * parts * parts * 600, bytes_accessed=8 << 20, transcendentals=0
            ),
            name="local_tiles",
        )(pairs, pair_count, state)

    state, *sends = pl.pallas_call(
        begin_kernel,
        out_shape=(state_shape,) + (send_shape,) * 4,
        in_specs=[smem] * 3 + [pl.BlockSpec(memory_space=pltpu.MemorySpace.HBM)] * 5,
        out_specs=(vmem,) * 5,
        scratch_shapes=[pltpu.VMEM((blocks, parts), f32), raw_scratch]
        + [pltpu.VMEM(a.shape, f32) for a in (position, velocity, stress, mass, density)]
        + [pltpu.SemaphoreType.DMA((5,))],
        compiler_params=params,
        name="begin",
    )(counts, lists, links, position, velocity, stress, mass, density)
    far = exchange(sends)
    behind_depth, behind_strip = pair_list(far[1]), pair_list(far[3])
    acc, right = local(state)
    half, *sends = pl.pallas_call(
        half_kernel,
        out_shape=(state_shape,) + (send_shape,) * 4,
        in_specs=[smem] * 5 + [vmem] * 10,
        out_specs=(vmem,) * 5,
        scratch_shapes=far_scratch + [raw_scratch],
        compiler_params=params,
        name="half_step",
    )(
        lists, links, behind_depth, behind_strip, contact,
        acc, right, *far, state, stress, plastic, cohesion,
    )
    far = exchange(sends)
    acc, right = local(half)
    outs = pl.pallas_call(
        end_kernel,
        out_shape=(
            shape(position.shape, f32),
            shape(velocity.shape, f32),
            shape(stress.shape, f32),
            shape(plastic.shape, f32),
        ),
        in_specs=[smem] * 5 + [vmem] * 12,
        out_specs=(vmem,) * 4,
        scratch_shapes=far_scratch,
        compiler_params=params,
        name="full_step",
    )(
        lists, links, behind_depth, behind_strip, contact,
        acc, right, *far, half, stress, plastic, cohesion, position, velocity,
    )
    return tuple(out[None, None] for out in outs)


def solution(mesh):
    def spec(rank):
        return P("strip", "depth", *([None] * (rank - 2)))

    return jax.shard_map(
        shards,
        mesh=mesh,
        in_specs=tuple(spec(r) for r in (5, 5, 5, 4, 4, 4, 4, 3, 4, 2, 4, 5, 3)),
        out_specs=tuple(spec(r) for r in (5, 5, 5, 4)),
        check_vma=False,
    )
```

```python
import jax
import jax.numpy as jnp
from jax import lax
from jax.experimental import pallas as pl
from jax.experimental.pallas import tpu as pltpu
from jax.sharding import PartitionSpec as P

RETURN_ITERS = 4

smooth_len = 1.5
kernel_coef = -105.0 / (3.141592653589793 * 1.5**5)
time_step = 0.25
gravity = 1.0
spin_rate = 2.0
blade_stiff = 4.0
bulk_mod = 2.0
shear_mod = 1.5
friction = 0.25
harden_scale = 0.05
harden_mod = 0.5
relax_rate = 0.7
tau_floor = 0.5
voigt_index = ((0, 3, 5), (3, 1, 4), (5, 4, 2))
voigt_pairs = ((0, 0), (1, 1), (2, 2), (0, 1), (1, 2), (0, 2))

STATE = 16
SOURCES = 26
ROWS = 32
FEATURES = 32
UNROLL = 16
FACE_UNROLL = 4
PITCH = 36
BEGIN_VMEM = 24
MESH = pl.DeviceIdType.MESH
f32 = jnp.float32
bf16 = jnp.bfloat16


def source_rows(x, v, s, mass, volume):
    rows = [mass]
    rows += [mass * x[k] for k in range(3)]
    rows += [mass * s[c] for c in range(6)]
    for k in range(3):
        i = voigt_index[k]
        rows.append(mass * (s[i[0]] * x[0] + s[i[1]] * x[1] + s[i[2]] * x[2]))
    rows.append(volume)
    rows += [volume * v[k] for k in range(3)]
    rows += [volume * x[k] for k in range(3)]
    for a, b in voigt_pairs:
        rows.append(volume * (0.5 * (v[a] * x[b] + v[b] * x[a])))
    return rows


def split3(value):
    high = value.astype(bf16).astype(f32)
    rest = value - high
    mid = rest.astype(bf16).astype(f32)
    low = (rest - mid).astype(bf16).astype(f32)
    return high, mid, low


PRODUCTS = ((0, 0), (0, 1), (1, 0), (1, 1), (0, 2), (2, 0))


def distance_rows(x, row_side, col_side):
    scaled = [x[k] * (1.0 / smooth_len) for k in range(3)]
    parts = [split3(y) for y in scaled]
    norm = split3(scaled[0] * scaled[0] + scaled[1] * scaled[1] + scaled[2] * scaled[2])
    one = jnp.ones_like(x[0])
    zero = jnp.zeros_like(x[0])
    left, right = [], []
    for k in range(3):
        for a, b in PRODUCTS:
            left.append(-2.0 * parts[k][a])
            right.append(parts[k][b])
    left += list(norm) + [one] * 3
    right += [one] * 3 + list(norm)
    fill = FEATURES - len(left)
    return (left + [zero] * fill if row_side else None, right + [zero] * fill if col_side else None)


def put_rows(ref, rows, start, count, stride):
    for k, row in enumerate(rows):
        ref[pl.ds(start * stride + k, count, stride=stride), :] = row


def get_row(ref, k, count, stride):
    return ref[pl.ds(k, count, stride=stride), :]


def close_kernel(left, right):
    squared = lax.dot_general(left, right, (((1,), (0,)), ((), ())), preferred_element_type=f32)
    squared = jnp.maximum(squared, 1e-30)
    near = jnp.maximum(1.0 - squared * lax.rsqrt(squared), 0.0)
    return (near * near * near).astype(bf16)


def fold(result):
    return result[:ROWS] + result[ROWS:]


def spread(sources, kernel):
    return fold(
        lax.dot_general(sources, kernel, (((1,), (0,)), ((), ())), preferred_element_type=f32)
    )


def pipelined(groups, width, prepare, apply, acc):
    for u in range(width):
        prepare(0, u, 0)

    def step(i, carry):
        for half in range(2):
            g = 2 * i + half
            found = []
            for u in range(width):
                found += apply(g, u, half)
                prepare(g + 1, u, 1 - half)
            for at, value in found:
                acc[at] += value
        return carry

    lax.fori_loop(0, (groups + 1) // 2, step, 0)


def store_sources(tmp, src, start, count):
    def one(b, carry):
        rows = tmp[pl.ds(b * PITCH, ROWS), :]
        high = rows.astype(bf16)
        src[start + b, 0:ROWS, :] = high
        src[start + b, ROWS : 2 * ROWS, :] = (rows - high.astype(f32)).astype(bf16)
        return carry

    lax.fori_loop(0, count, one, 0, unroll=4)


def store_cols(tmp, col, start, count):
    def one(b, carry):
        col[start + b] = tmp[pl.ds(b * PITCH, FEATURES), :].astype(bf16)
        return carry

    lax.fori_loop(0, count, one, 0, unroll=4)


def store_lefts(tmp, left, start, count):
    def one(b, carry):
        left[start + b] = tmp[pl.ds(b * PITCH, FEATURES), :].T.astype(bf16)
        return carry

    lax.fori_loop(0, count, one, 0, unroll=4)


def gather_rims(rows, raw, lists, sends, after):
    for k, row in enumerate(rows):
        raw[:, k, :] = row
    for face in range(4):
        for slot in range(lists.shape[1]):
            sends[face, slot * STATE : (slot + 1) * STATE, :] = raw[lists[face, slot]]
        after(face)


class Faces:
    def __init__(self):
        d, n = lax.axis_index("depth"), lax.axis_size("depth")
        s, m = lax.axis_index("strip"), lax.axis_size("strip")
        self.there = (d < n - 1, d > 0, None, None)
        self.device = (
            {"depth": d + 1}, {"depth": d - 1},
            {"strip": lax.rem(s + 1, m)}, {"strip": lax.rem(s + m - 1, m)},
        )

    def when(self, face, act):
        if self.there[face] is None:
            act()
        else:
            pl.when(self.there[face])(act)

    def greet(self):
        barrier = pltpu.get_barrier_semaphore()
        for face in range(4):
            def act(face=face):
                pl.semaphore_signal(barrier, inc=1, device_id=self.device[face], device_id_type=MESH)
            self.when(face, act)

    def meet(self):
        peers = sum(1 if there is None else there.astype(jnp.int32) for there in self.there)
        pl.semaphore_wait(pltpu.get_barrier_semaphore(), peers)

    def copy(self, face, source, target, sent, got):
        return pltpu.make_async_remote_copy(
            src_ref=source, dst_ref=target, send_sem=sent, recv_sem=got,
            device_id=self.device[face], device_id_type=MESH,
        )


def prepare_local(rows, src, right, left, tmp, blocks):
    zero = jnp.zeros_like(rows[0])
    sources = source_rows(rows[0:3], rows[3:6], rows[6:12], rows[12], rows[13])
    put_rows(tmp, sources + [zero] * (ROWS - SOURCES), 0, blocks, PITCH)
    store_sources(tmp, src, 0, blocks)
    left_rows, right_rows = distance_rows(rows[0:3], True, True)
    put_rows(tmp, right_rows, 0, blocks, PITCH)
    store_cols(tmp, right, 0, blocks)
    put_rows(tmp, left_rows, 0, blocks, PITCH)
    store_lefts(tmp, left, 0, blocks)
    src[blocks] = jnp.zeros(src.shape[1:], bf16)
    right[blocks] = jnp.zeros(right.shape[1:], bf16)
    left[blocks] = jnp.zeros(left.shape[1:], bf16)


def prepare_far(far, f, src, left, tmp, rim):
    got = [get_row(far.at[f], k, rim, STATE) for k in range(14)]
    zero = jnp.zeros_like(got[0])
    rows = source_rows(got[0:3], got[3:6], got[6:12], got[12], got[13])
    put_rows(tmp, rows + [zero] * (ROWS - SOURCES), 0, rim, PITCH)
    store_sources(tmp, src, f * rim, rim)
    put_rows(tmp, distance_rows(got[0:3], True, False)[0], 0, rim, PITCH)
    store_lefts(tmp, left, f * rim, rim)


def share(faces, rows, lists, raw, sends, far, sent, got, src, right, left, far_src, far_left, tmp, extra):
    blocks, rim = rows[0].shape[0], lists.shape[1]
    copies = [
        faces.copy(face, sends.at[face], far.at[face ^ 1], sent.at[face], got.at[face ^ 1])
        for face in range(4)
    ]

    def after(face):
        if face == 0:
            faces.meet()
        faces.when(face, copies[face].start)

    gather_rims(rows, raw, lists, sends, after)
    extra()
    prepare_local(rows, src, right, left, tmp, blocks)
    far_src[4 * rim] = jnp.zeros(far_src.shape[1:], bf16)
    far_left[4 * rim] = jnp.zeros(far_left.shape[1:], bf16)
    for face in (2, 3, 0, 1):
        if faces.there[face] is not None:
            @pl.when(jnp.logical_not(faces.there[face]))
            def _():
                far[face] = jnp.zeros(far.shape[1:], f32)
        faces.when(face, copies[face ^ 1].wait_recv)
        prepare_far(far, face, far_src, far_left, tmp, rim)
    for face in range(4):
        faces.when(face, copies[face].wait_send)


def begin_kernel(
    counts_in, lists_in, links_in, pairs_in, contact_in, pos_in, vel_in, stress_in, mass_in, density_in,
    plastic_in, cohesion_in,
    state, src, right, left, far_src, far_left, behind_depth, behind_strip,
    stress, plastic, cohesion, lists_out, links_out, pairs, contact,
    counts, lists, links, occ, raw, pos, vel, mass, density, sends, far, tmp, packed,
    sems, sent, got, pack_sent, pack_got,
):
    faces = Faces()
    faces.greet()
    moved = (
        (counts_in, counts), (lists_in, lists), (pos_in, pos), (vel_in, vel), (stress_in, stress),
        (mass_in, mass), (density_in, density), (links_in, links),
        (plastic_in, plastic), (cohesion_in, cohesion),
        (lists_in, lists_out), (links_in, links_out), (pairs_in, pairs), (contact_in, contact),
    )
    copies = [pltpu.make_async_copy(a, b, sems.at[i]) for i, (a, b) in enumerate(moved)]
    for copy in copies:
        copy.start()
    blocks, parts = mass.shape
    lane = lax.broadcasted_iota(jnp.int32, (1, parts), 1)
    packed[...] = jnp.zeros(packed.shape, jnp.int32)
    copies[0].wait()
    for b in range(blocks):
        occ[b : b + 1, :] = jnp.where(lane < counts[0, b], 1.0, 0.0)
    live = occ[...]
    for copy in copies[1:7]:
        copy.wait()
    rho = density[...]
    inverse = 1.0 / (rho * rho)
    weighted = mass[...] * live * kernel_coef
    rows = [pos[k] for k in range(3)] + [vel[k] for k in range(3)]
    rows += [stress[c] * inverse for c in range(6)]
    rows += [weighted, weighted / rho, live, inverse]
    for k, row in enumerate(rows):
        state[k] = row
    packs = (
        faces.copy(0, packed.at[0], behind_depth, pack_sent.at[0], pack_got.at[0]),
        faces.copy(2, packed.at[1], behind_strip, pack_sent.at[1], pack_got.at[1]),
    )

    def extra():
        copies[7].wait()
        for face in range(2):
            for side in range(2):
                row = jnp.zeros((1, parts), jnp.int32)
                for q in range(links.shape[2]):
                    row = jnp.where(lane == q, links[face, side, q], row)
                packed[face, side : side + 1, :] = row
            faces.when(2 * face, packs[face].start)

    share(
        faces, rows, lists, raw, sends, far, sent, got, src, right, left, far_src, far_left, tmp, extra
    )

    @pl.when(jnp.logical_not(faces.there[1]))
    def _():
        behind_depth[...] = jnp.zeros(behind_depth.shape, jnp.int32)

    faces.when(1, packs[0].wait_recv)
    packs[1].wait_recv()
    faces.when(0, packs[0].wait_send)
    packs[1].wait_send()
    for copy in copies[8:]:
        copy.wait()


def again_kernel(
    lists, state, src, right, left, far_src, far_left, raw, sends, far, tmp, sent, got
):
    faces = Faces()
    faces.greet()
    rows = [state[k] for k in range(STATE)]
    share(
        faces, rows, lists, raw, sends, far, sent, got, src, right, left, far_src, far_left, tmp,
        lambda: None,
    )


def local_sums(pairs, total, src, right, left, acc, held, turned):
    blocks = src.shape[0] - 1
    live = total[0, 0]
    last = pairs.shape[1] - 1

    def entry(q):
        at = jnp.minimum(q, last)
        a, b = pairs[0, at], pairs[1, at]
        return jnp.where(q < live, a, blocks), jnp.where(q < live, b, blocks)

    def prepare(g, u, slot):
        a, b = entry(g * UNROLL + u)
        kernel = close_kernel(left[a], right[b])
        held[slot * UNROLL + u] = kernel
        turned[slot * UNROLL + u] = kernel.T

    def apply(g, u, slot):
        a, b = entry(g * UNROLL + u)
        at = slot * UNROLL + u
        other = jnp.where(a == b, blocks, b)
        return [(a, spread(src[b], turned[at])), (other, spread(src[a], held[at]))]

    pipelined((live + UNROLL - 1) // UNROLL, UNROLL, prepare, apply, acc)


def cross_sums(lists, links, links_behind, src, right, left, acc, held):
    rim = lists.shape[1]
    cross = links.shape[2]
    whole = cross % (2 * FACE_UNROLL) == 0

    def entry(g, u):
        q = g * FACE_UNROLL + u // 4
        at = jnp.minimum(q, cross - 1)
        face, behind = (u % 4) // 2, u % 2
        if behind:
            own = lists[2 * face + 1, links_behind[face][1, at]]
            far_slot = links_behind[face][0, at]
        else:
            own, far_slot = lists[2 * face, links[face, 0, at]], links[face, 1, at]
        far_slot = (u % 4) * rim + far_slot
        return own, far_slot if whole else jnp.where(q < cross, far_slot, 4 * rim)

    width = 4 * FACE_UNROLL

    def prepare(g, u, slot):
        own, far_slot = entry(g, u)
        held[slot * width + u] = close_kernel(left[far_slot], right[own])

    def apply(g, u, slot):
        own, far_slot = entry(g, u)
        return [(own, spread(src[far_slot], held[slot * width + u]))]

    pipelined((cross + FACE_UNROLL - 1) // FACE_UNROLL, width, prepare, apply, acc)


def section_rates(summed, x, v, s, contact_flag):
    blade = (spin_rate * x[2], jnp.zeros_like(x[1]), -spin_rate * x[0])
    acceleration = []
    arm = [x[l] * summed[0] - summed[1 + l] for l in range(3)]
    for k in range(3):
        total = -summed[10 + k] + blade_stiff * contact_flag * (blade[k] - v[k])
        for l in range(3):
            slot = voigt_index[k][l]
            total = total + s[slot] * arm[l] + x[l] * summed[4 + slot]
        if k == 2:
            total = total - gravity
        acceleration.append(total)
    strain = []
    for c, (k, l) in enumerate(voigt_pairs):
        rate = 0.5 * (x[l] * summed[14 + k] + x[k] * summed[14 + l]) - summed[20 + c]
        rate = rate - 0.5 * summed[13] * (v[k] * x[l] + v[l] * x[k])
        rate = rate + 0.5 * (v[k] * summed[17 + l] + v[l] * summed[17 + k])
        strain.append(rate)
    return acceleration, strain


def elastic_step(stress, strain, fraction):
    volumetric = strain[0] + strain[1] + strain[2]
    lame_first = bulk_mod - 2.0 * shear_mod / 3.0
    components = []
    for c in range(6):
        change = 2.0 * shear_mod * strain[c]
        if c < 3:
            change = change + lame_first * volumetric
        components.append(stress[c] + fraction * time_step * change)
    return components


def plastic_return(c, plastic, cohesion):
    for _ in range(RETURN_ITERS):
        mean = (c[0] + c[1] + c[2]) / 3.0
        d = [c[0] - mean, c[1] - mean, c[2] - mean, c[3], c[4], c[5]]
        second = 0.5 * (d[0] * d[0] + d[1] * d[1] + d[2] * d[2])
        second = second + d[3] * d[3] + d[4] * d[4] + d[5] * d[5]
        tau = jnp.sqrt(second)
        limit = cohesion * (1.0 + plastic / (plastic + harden_scale))
        excess = jnp.maximum(tau + friction * 3.0 * mean - limit, 0.0)
        multiplier = (
            relax_rate * excess / (shear_mod + 9.0 * bulk_mod * friction * friction + harden_mod)
        )
        shrink = jnp.maximum(1.0 - shear_mod * multiplier / jnp.maximum(tau, tau_floor), 0.0)
        mean = mean - 3.0 * bulk_mod * friction * multiplier
        c = [
            d[0] * shrink + mean,
            d[1] * shrink + mean,
            d[2] * shrink + mean,
            d[3] * shrink,
            d[4] * shrink,
            d[5] * shrink,
        ]
        plastic = plastic + multiplier
    return c, plastic


def contact_rows(contact, flag, blocks):
    flag[...] = jnp.zeros_like(flag)
    for i in range(contact.shape[1]):
        flag[pl.ds(contact[0, i], 1), :] += 1.0
    return flag[0:blocks, :]


def rates_of(acc, state, contact, flag):
    blocks, parts = state.shape[1:]
    contact_flag = contact_rows(contact, flag, blocks)
    x = [state[k] for k in range(3)]
    v = [state[k] for k in range(3, 6)]
    s = [state[k] for k in range(6, 12)]
    summed = [acc[0:blocks, k, :] for k in range(SOURCES)]
    return x, v, *section_rates(summed, x, v, s, contact_flag)


def sums(pairs, total, lists, links, behind, src, right, left, far_src, far_left, acc, held, turned):
    acc[...] = jnp.zeros(acc.shape, f32)
    local_sums(pairs, total, src, right, left, acc, held, turned)
    cross_sums(lists, links, behind, far_src, right, far_left, acc, held)


def half_kernel(
    pairs, total, lists, links, behind_depth, behind_strip, contact,
    src, right, left, far_src, far_left, state, stress, plastic, cohesion,
    state_out,
    acc, held, turned, flag,
):
    sums(
        pairs, total, lists, links, (behind_depth, behind_strip),
        src, right, left, far_src, far_left, acc, held, turned,
    )
    x, v, acceleration, strain = rates_of(acc, state, contact, flag)
    components, _ = plastic_return(
        elastic_step([stress[c] for c in range(6)], strain, 0.5), plastic[...], cohesion[...]
    )
    inverse = state[15]
    rows = [x[k] + 0.5 * time_step * v[k] for k in range(3)]
    rows += [v[k] + 0.5 * time_step * acceleration[k] for k in range(3)]
    rows += [c * inverse for c in components]
    rows += [state[12], state[13], state[14], inverse]
    for k, row in enumerate(rows):
        state_out[k] = row


def end_kernel(
    pairs, total, lists, links, behind_depth, behind_strip, contact,
    src, right, left, far_src, far_left, state, stress, plastic, cohesion, first,
    new_position, new_velocity, new_stress, new_plastic,
    acc, held, turned, flag,
):
    sums(
        pairs, total, lists, links, (behind_depth, behind_strip),
        src, right, left, far_src, far_left, acc, held, turned,
    )
    _, half_v, acceleration, strain = rates_of(acc, state, contact, flag)
    components, hardened = plastic_return(
        elastic_step([stress[c] for c in range(6)], strain, 1.0), plastic[...], cohesion[...]
    )
    live = state[14]
    for k in range(3):
        new_position[k] = (first[k] + time_step * half_v[k]) * live
        new_velocity[k] = (first[3 + k] + time_step * acceleration[k]) * live
    for c in range(6):
        new_stress[c] = components[c] * live
    new_plastic[...] = hardened * live


def shards(
    position, velocity, stress, plastic, particle_mass, density, cohesion,
    counts, block_pairs, pair_count, send_lists, cross_links, contact,
):
    position, velocity, stress = position[0, 0], velocity[0, 0], stress[0, 0]
    plastic, mass, density, cohesion = plastic[0, 0], particle_mass[0, 0], density[0, 0], cohesion[0, 0]
    counts, pairs, lists = counts[0], jnp.swapaxes(block_pairs[0, 0], 0, 1), send_lists[0, 0]
    links, contact = jnp.swapaxes(cross_links[0, 0], 1, 2), contact[0]
    blocks, parts = mass.shape
    rim = lists.shape[1]
    smem = pl.BlockSpec(memory_space=pltpu.SMEM)
    vmem = pl.BlockSpec(memory_space=pltpu.VMEM)
    hbm = pl.BlockSpec(memory_space=pltpu.MemorySpace.HBM)
    shape = jax.ShapeDtypeStruct
    i32 = jnp.int32

    def like(a):
        return shape(a.shape, a.dtype)

    state_shape = shape((STATE, blocks, parts), f32)
    ready = (
        shape((blocks + 1, 2 * ROWS, parts), bf16),
        shape((blocks + 1, FEATURES, parts), bf16),
        shape((blocks + 1, parts, FEATURES), bf16),
        shape((4 * rim + 1, 2 * ROWS, parts), bf16),
        shape((4 * rim + 1, parts, FEATURES), bf16),
    )
    behind_shape = shape((8, parts), i32)
    rims = pltpu.VMEM((4, rim * STATE, parts), f32)
    raw = pltpu.VMEM((blocks, STATE, parts), f32)
    tmp = pltpu.VMEM((max(blocks, rim) * PITCH, parts), f32)
    dma = pltpu.SemaphoreType.DMA
    width = max(2 * UNROLL, 8 * FACE_UNROLL)
    tile_scratch = [
        pltpu.VMEM((blocks + 1, ROWS, parts), f32),
        pltpu.VMEM((width, parts, parts), bf16),
        pltpu.VMEM((2 * UNROLL, parts, parts), bf16),
        pltpu.VMEM((blocks + 8, parts), f32),
    ]
    params = pltpu.CompilerParams(vmem_limit_bytes=24 << 20)

    state, *rest = pl.pallas_call(
        begin_kernel,
        out_shape=(state_shape,) + ready + (behind_shape, behind_shape)
        + tuple(like(a) for a in (stress, plastic, cohesion, lists, links, pairs, contact)),
        in_specs=[hbm] * 12,
        out_specs=(vmem,) * 15,
        scratch_shapes=[pltpu.SMEM(a.shape, i32) for a in (counts, lists, links)]
        + [pltpu.VMEM((blocks, parts), f32), raw]
        + [pltpu.VMEM(a.shape, f32) for a in (position, velocity, mass, density)]
        + [rims, rims, tmp, pltpu.VMEM((2, 8, parts), i32)]
        + [dma((14,)), dma((4,)), dma((4,)), dma((2,)), dma((2,))],
        compiler_params=pltpu.CompilerParams(
            vmem_limit_bytes=BEGIN_VMEM << 20, collective_id=0, has_side_effects=True
        ),
        name="begin",
    )(*(
        pltpu.with_memory_space_constraint(a, pltpu.MemorySpace.HBM)
        for a in (counts, lists, links, pairs, contact, position, velocity, stress, mass, density, plastic, cohesion)
    ))
    prepared, rest = rest[:5], rest[5:]
    behind, (stress_v, plastic_v, cohesion_v, lists_v, links_v, pairs_v, contact_v) = rest[:2], rest[2:]
    ints = (pairs_v, pair_count, lists_v, links_v, *behind, contact_v)
    cost = pl.CostEstimate(flops=pairs.shape[1] * parts * parts * 1000, bytes_accessed=8 << 20, transcendentals=0)
    half = pl.pallas_call(
        half_kernel,
        out_shape=state_shape,
        in_specs=[smem] * 7 + [vmem] * 9,
        out_specs=vmem,
        scratch_shapes=tile_scratch,
        compiler_params=params,
        cost_estimate=cost,
        name="half_step",
    )(*ints, *prepared, state, stress_v, plastic_v, cohesion_v)
    prepared = pl.pallas_call(
        again_kernel,
        out_shape=ready,
        in_specs=[smem, vmem],
        out_specs=(vmem,) * 5,
        scratch_shapes=[raw, rims, rims, tmp, dma((4,)), dma((4,))],
        compiler_params=pltpu.CompilerParams(
            vmem_limit_bytes=24 << 20, collective_id=1, has_side_effects=True
        ),
        name="again",
    )(lists_v, half)
    outs = pl.pallas_call(
        end_kernel,
        out_shape=(
            shape(position.shape, f32), shape(velocity.shape, f32), shape(stress.shape, f32), shape(plastic.shape, f32)
        ),
        in_specs=[smem] * 7 + [vmem] * 10,
        out_specs=(vmem,) * 4,
        scratch_shapes=tile_scratch,
        compiler_params=params,
        cost_estimate=cost,
        name="full_step",
    )(*ints, *prepared, half, stress_v, plastic_v, cohesion_v, state)
    return tuple(out[None, None] for out in outs)


def solution(mesh):
    def spec(rank):
        return P("strip", "depth", *([None] * (rank - 2)))

    return jax.shard_map(
        shards,
        mesh=mesh,
        in_specs=tuple(spec(r) for r in (5, 5, 5, 4, 4, 4, 4, 3, 4, 2, 4, 5, 3)),
        out_specs=tuple(spec(r) for r in (5, 5, 5, 4)),
        check_vma=False,
    )
```

```python
import jax
import jax.numpy as jnp
from jax import lax
from jax.experimental import pallas as pl
from jax.experimental.pallas import tpu as pltpu
from jax.sharding import PartitionSpec as P

RETURN_ITERS = 4

smooth_len = 1.5
kernel_coef = -105.0 / (3.141592653589793 * 1.5**5)
time_step = 0.25
gravity = 1.0
spin_rate = 2.0
blade_stiff = 4.0
bulk_mod = 2.0
shear_mod = 1.5
friction = 0.25
harden_scale = 0.05
harden_mod = 0.5
relax_rate = 0.7
tau_floor = 0.5
voigt_index = ((0, 3, 5), (3, 1, 4), (5, 4, 2))
voigt_pairs = ((0, 0), (1, 1), (2, 2), (0, 1), (1, 2), (0, 2))

STATE = 16
SOURCES = 26
ROWS = 32
FEATURES = 32
UNROLL = 16
FACE_UNROLL = 4
PITCH = 36
LIVE_ROWS = 14
MOVING_ROWS = 12
ACC_PITCH = 40
MESH = pl.DeviceIdType.MESH
f32 = jnp.float32
bf16 = jnp.bfloat16


def source_rows(x, v, s, mass, volume):
    rows = [mass]
    rows += [mass * x[k] for k in range(3)]
    rows += [mass * s[c] for c in range(6)]
    for k in range(3):
        i = voigt_index[k]
        rows.append(mass * (s[i[0]] * x[0] + s[i[1]] * x[1] + s[i[2]] * x[2]))
    rows.append(volume)
    rows += [volume * v[k] for k in range(3)]
    rows += [volume * x[k] for k in range(3)]
    for a, b in voigt_pairs:
        rows.append(volume * (0.5 * (v[a] * x[b] + v[b] * x[a])))
    return rows


def split3(value):
    high = value.astype(bf16).astype(f32)
    rest = value - high
    mid = rest.astype(bf16).astype(f32)
    low = (rest - mid).astype(bf16).astype(f32)
    return high, mid, low


PRODUCTS = ((0, 0), (0, 1), (1, 0), (1, 1), (0, 2), (2, 0))


def distance_rows(x, row_side, col_side):
    scaled = [x[k] * (1.0 / smooth_len) for k in range(3)]
    parts = [split3(y) for y in scaled]
    norm = split3(scaled[0] * scaled[0] + scaled[1] * scaled[1] + scaled[2] * scaled[2])
    one = jnp.ones_like(x[0])
    zero = jnp.zeros_like(x[0])
    left, right = [], []
    for k in range(3):
        for a, b in PRODUCTS:
            left.append(-2.0 * parts[k][a])
            right.append(parts[k][b])
    left += list(norm) + [one] * 3
    right += [one] * 3 + list(norm)
    fill = FEATURES - len(left)
    return (left + [zero] * fill if row_side else None, right + [zero] * fill if col_side else None)


def put_rows(ref, rows, start, count, stride):
    for k, row in enumerate(rows):
        ref[pl.ds(start * stride + k, count, stride=stride), :] = row


def get_row(ref, k, count, stride):
    return ref[pl.ds(k, count, stride=stride), :]


def close_kernel(left, right):
    squared = lax.dot_general(left, right, (((1,), (0,)), ((), ())), preferred_element_type=f32)
    squared = jnp.maximum(squared, 1e-30)
    near = jnp.maximum(1.0 - squared * lax.rsqrt(squared), 0.0)
    return (near * near * near).astype(bf16)


def fold(result):
    return result[:ROWS] + result[ROWS:]


def spread(sources, kernel):
    return fold(
        lax.dot_general(sources, kernel, (((1,), (0,)), ((), ())), preferred_element_type=f32)
    )


def pipelined(steps, width, prepare, apply, finish):
    for u in range(width):
        prepare(0, u, 0)

    def step(i, carry):
        for half in range(2):
            g = 2 * i + half
            found = []
            for u in range(width):
                found += apply(g, u, half)
                prepare(g + 1, u, 1 - half)
            finish(g, found)
        return carry

    lax.fori_loop(0, steps, step, 0)


def split_sources(tmp, b):
    rows = tmp[pl.ds(b * PITCH, ROWS), :]
    high = rows.astype(bf16)
    return high, (rows - high.astype(f32)).astype(bf16)


def store_features(tmps, src, right, left, start, count):
    def one(b, carry):
        high, low = split_sources(tmps[0], b)
        src[start + b, 0:ROWS, :] = high
        src[start + b, ROWS : 2 * ROWS, :] = low
        left[start + b] = tmps[1][pl.ds(b * PITCH, FEATURES), :].T.astype(bf16)
        if right is not None:
            right[start + b] = tmps[2][pl.ds(b * PITCH, FEATURES), :].astype(bf16)
        return carry

    lax.fori_loop(0, count, one, 0, unroll=8)


def gather_rims(rows, raw, lists, sends, after):
    for k, row in enumerate(rows):
        raw[:, k, :] = row
    width = len(rows)
    for face in range(4):
        for slot in range(lists.shape[1]):
            sends[face, slot * width : (slot + 1) * width, :] = raw[lists[face, slot]][:width]
        after(face)


class Faces:
    def __init__(self):
        d, n = lax.axis_index("depth"), lax.axis_size("depth")
        s, m = lax.axis_index("strip"), lax.axis_size("strip")
        self.there = (d < n - 1, d > 0, None, None)
        self.device = (
            {"depth": d + 1}, {"depth": d - 1},
            {"strip": lax.rem(s + 1, m)}, {"strip": lax.rem(s + m - 1, m)},
        )

    def when(self, face, act):
        if self.there[face] is None:
            act()
        else:
            pl.when(self.there[face])(act)

    def greet(self):
        barrier = pltpu.get_barrier_semaphore()
        for face in range(4):
            def act(face=face):
                pl.semaphore_signal(barrier, inc=1, device_id=self.device[face], device_id_type=MESH)
            self.when(face, act)

    def meet(self):
        peers = sum(1 if there is None else there.astype(jnp.int32) for there in self.there)
        pl.semaphore_wait(pltpu.get_barrier_semaphore(), peers)

    def copy(self, face, source, target, sent, got):
        return pltpu.make_async_remote_copy(
            src_ref=source, dst_ref=target, send_sem=sent, recv_sem=got,
            device_id=self.device[face], device_id_type=MESH,
        )


def prepare_local(rows, src, right, left, tmps, blocks):
    zero = jnp.zeros_like(rows[0])
    sources = source_rows(rows[0:3], rows[3:6], rows[6:12], rows[12], rows[13])
    put_rows(tmps[0], sources + [zero] * (ROWS - SOURCES), 0, blocks, PITCH)
    left_rows, right_rows = distance_rows(rows[0:3], True, True)
    put_rows(tmps[1], left_rows, 0, blocks, PITCH)
    put_rows(tmps[2], right_rows, 0, blocks, PITCH)
    store_features(tmps, src, right, left, 0, blocks)
    src[blocks] = jnp.zeros(src.shape[1:], bf16)
    right[blocks] = jnp.zeros(right.shape[1:], bf16)
    left[blocks] = jnp.zeros(left.shape[1:], bf16)


def prepare_far(got, f, src, left, tmps, rim):
    zero = jnp.zeros_like(got[0])
    rows = source_rows(got[0:3], got[3:6], got[6:12], got[12], got[13])
    put_rows(tmps[0], rows + [zero] * (ROWS - SOURCES), 0, rim, PITCH)
    put_rows(tmps[1], distance_rows(got[0:3], True, False)[0], 0, rim, PITCH)
    store_features(tmps, src, None, left, f * rim, rim)


def pair_at(pairs, live, q, blocks):
    at = jnp.minimum(q, pairs.shape[1] - 1)
    a, b = pairs[0, at], pairs[1, at]
    return jnp.where(q < live, a, blocks), jnp.where(q < live, b, blocks)


def local_terms(pairs, total, src, right, left, terms, held, turned):
    blocks = src.shape[0] - 1
    live = total[0, 0]

    def prepare(g, u, slot):
        a, b = pair_at(pairs, live, g * UNROLL + u, blocks)
        kernel = close_kernel(left[a], right[b])
        held[slot * UNROLL + u] = kernel
        turned[slot * UNROLL + u] = kernel.T

    def apply(g, u, slot):
        q = g * UNROLL + u
        a, b = pair_at(pairs, live, q, blocks)
        at = slot * UNROLL + u
        return [(q, 0, spread(src[b], turned[at])), (q, 1, spread(src[a], held[at]))]

    def finish(g, found):
        for q, side, value in found:
            terms[q, side] = value

    pipelined(terms.shape[0] // (2 * UNROLL), UNROLL, prepare, apply, finish)


def share(
    faces, rows, sent_rows, far_mass, lists, pairs, total, raw, sends, far, sent, got,
    right, far_src, far_left, terms, src, left, held, turned, tmps, extra,
):
    blocks, rim = rows[0].shape[0], lists.shape[1]
    copies = [
        faces.copy(face, sends.at[face], far.at[face ^ 1], sent.at[face], got.at[face ^ 1])
        for face in range(4)
    ]

    def after(face):
        if face == 0:
            faces.meet()
        faces.when(face, copies[face].start)

    gather_rims(rows[:sent_rows], raw, lists, sends, after)
    extra()
    prepare_local(rows, src, right, left, tmps, blocks)
    local_terms(pairs, total, src, right, left, terms, held, turned)
    far_src[4 * rim] = jnp.zeros(far_src.shape[1:], bf16)
    far_left[4 * rim] = jnp.zeros(far_left.shape[1:], bf16)
    for face in (2, 3, 0, 1):
        if faces.there[face] is not None:
            @pl.when(jnp.logical_not(faces.there[face]))
            def _():
                far[face] = jnp.zeros(far.shape[1:], f32)
        faces.when(face, copies[face ^ 1].wait_recv)
        arrived = [get_row(far.at[face], k, rim, sent_rows) for k in range(sent_rows)]
        if sent_rows == LIVE_ROWS:
            far_mass[face, 0], far_mass[face, 1] = arrived[12], arrived[13]
        else:
            arrived += [far_mass[face, 0], far_mass[face, 1]]
        prepare_far(arrived, face, far_src, far_left, tmps, rim)
    for face in range(4):
        faces.when(face, copies[face].wait_send)


def begin_kernel(
    total, counts_in, lists_in, links_in, pairs_in, contact_in, pos_in, vel_in, stress_in, mass_in, density_in,
    plastic_in, cohesion_in,
    state, right, far_src, far_left, terms, far_mass, behind_depth, behind_strip,
    stress, plastic, cohesion, lists_out, links_out, pairs_out, contact,
    counts, lists, links, pairs, occ, pos, vel, mass, density, packed,
    sems, pack_sent, pack_got,
    raw, sends, far, src, left, held, turned, tmp0, tmp1, tmp2, sent, got,
):
    faces = Faces()
    faces.greet()
    moved = (
        (counts_in, counts), (lists_in, lists), (pos_in, pos), (vel_in, vel), (stress_in, stress),
        (mass_in, mass), (density_in, density), (links_in, links),
        (plastic_in, plastic), (cohesion_in, cohesion),
        (lists_in, lists_out), (links_in, links_out), (pairs_in, pairs_out), (contact_in, contact),
        (pairs_in, pairs),
    )
    copies = [pltpu.make_async_copy(a, b, sems.at[i]) for i, (a, b) in enumerate(moved)]
    for copy in copies:
        copy.start()
    blocks, parts = mass.shape
    lane = lax.broadcasted_iota(jnp.int32, (1, parts), 1)
    packed[...] = jnp.zeros(packed.shape, jnp.int32)
    copies[0].wait()
    for b in range(blocks):
        occ[b : b + 1, :] = jnp.where(lane < counts[0, b], 1.0, 0.0)
    live = occ[...]
    for copy in copies[1:7] + copies[14:]:
        copy.wait()
    rho = density[...]
    inverse = 1.0 / (rho * rho)
    weighted = mass[...] * live * kernel_coef
    rows = [pos[k] for k in range(3)] + [vel[k] for k in range(3)]
    rows += [stress[c] * inverse for c in range(6)]
    rows += [weighted, weighted / rho, live, inverse]
    for k, row in enumerate(rows):
        state[k] = row
    packs = (
        faces.copy(0, packed.at[0], behind_depth, pack_sent.at[0], pack_got.at[0]),
        faces.copy(2, packed.at[1], behind_strip, pack_sent.at[1], pack_got.at[1]),
    )

    def extra():
        copies[7].wait()
        for face in range(2):
            for side in range(2):
                row = jnp.zeros((1, parts), jnp.int32)
                for q in range(links.shape[2]):
                    row = jnp.where(lane == q, links[face, side, q], row)
                packed[face, side : side + 1, :] = row
            faces.when(2 * face, packs[face].start)

    share(
        faces, rows, LIVE_ROWS, far_mass, lists, pairs, total, raw, sends, far, sent, got,
        right, far_src, far_left, terms, src, left, held, turned, (tmp0, tmp1, tmp2), extra,
    )

    @pl.when(jnp.logical_not(faces.there[1]))
    def _():
        behind_depth[...] = jnp.zeros(behind_depth.shape, jnp.int32)

    faces.when(1, packs[0].wait_recv)
    packs[1].wait_recv()
    faces.when(0, packs[0].wait_send)
    packs[1].wait_send()
    for copy in copies[8:14]:
        copy.wait()


def again_kernel(
    total, lists, pairs, state, far_mass, right, far_src, far_left, terms,
    raw, sends, far, src, left, held, turned, tmp0, tmp1, tmp2, sent, got,
):
    faces = Faces()
    faces.greet()
    rows = [state[k] for k in range(STATE)]
    share(
        faces, rows, MOVING_ROWS, far_mass, lists, pairs, total, raw, sends, far, sent, got,
        right, far_src, far_left, terms, src, left, held, turned, (tmp0, tmp1, tmp2),
        lambda: None,
    )


def add_block(acc, at, value):
    rows = pl.ds(pl.multiple_of(at * ACC_PITCH, 8), ROWS)
    acc[rows, :] += value


def sums(pairs, total, lists, links, links_behind, right, src, left, terms, acc, own_acc, held):
    acc[...] = jnp.zeros(acc.shape, f32)
    own_acc[...] = jnp.zeros(own_acc.shape, f32)
    rim = lists.shape[1]
    blocks = right.shape[0] - 1
    live = total[0, 0]
    cross = links.shape[2]
    whole = cross % (2 * FACE_UNROLL) == 0

    def entry(g, u):
        q = g * FACE_UNROLL + u // 4
        at = jnp.minimum(q, cross - 1)
        face, behind = (u % 4) // 2, u % 2
        if behind:
            own = lists[2 * face + 1, links_behind[face][1, at]]
            far_slot = links_behind[face][0, at]
        else:
            own, far_slot = lists[2 * face, links[face, 0, at]], links[face, 1, at]
        far_slot = (u % 4) * rim + far_slot
        return own, far_slot if whole else jnp.where(q < cross, far_slot, 4 * rim)

    width = 4 * FACE_UNROLL

    def prepare(g, u, slot):
        own, far_slot = entry(g, u)
        held[slot * width + u] = close_kernel(left[far_slot], right[own])

    def apply(g, u, slot):
        own, far_slot = entry(g, u)
        return [(own, spread(src[far_slot], held[slot * width + u]))]

    steps = (cross + 2 * FACE_UNROLL - 1) // (2 * FACE_UNROLL)
    count = pairs.shape[1]
    share_of = (count + 2 * steps - 1) // (2 * steps)

    def finish(g, found):
        for u in range(share_of):
            q = g * share_of + u
            a, b = pair_at(pairs, live, q, blocks)
            at = jnp.minimum(q, count - 1)
            add_block(own_acc, a, terms[at, 0])
            add_block(own_acc, jnp.where(a == b, blocks, b), terms[at, 1])
        for at, value in found:
            add_block(acc, at, value)

    pipelined(steps, width, prepare, apply, finish)


def section_rates(summed, x, v, s, contact_flag):
    blade = (spin_rate * x[2], jnp.zeros_like(x[1]), -spin_rate * x[0])
    acceleration = []
    arm = [x[l] * summed[0] - summed[1 + l] for l in range(3)]
    for k in range(3):
        total = -summed[10 + k] + blade_stiff * contact_flag * (blade[k] - v[k])
        for l in range(3):
            slot = voigt_index[k][l]
            total = total + s[slot] * arm[l] + x[l] * summed[4 + slot]
        if k == 2:
            total = total - gravity
        acceleration.append(total)
    strain = []
    for c, (k, l) in enumerate(voigt_pairs):
        rate = 0.5 * (x[l] * summed[14 + k] + x[k] * summed[14 + l]) - summed[20 + c]
        rate = rate - 0.5 * summed[13] * (v[k] * x[l] + v[l] * x[k])
        rate = rate + 0.5 * (v[k] * summed[17 + l] + v[l] * summed[17 + k])
        strain.append(rate)
    return acceleration, strain


def elastic_step(stress, strain, fraction):
    volumetric = strain[0] + strain[1] + strain[2]
    lame_first = bulk_mod - 2.0 * shear_mod / 3.0
    components = []
    for c in range(6):
        change = 2.0 * shear_mod * strain[c]
        if c < 3:
            change = change + lame_first * volumetric
        components.append(stress[c] + fraction * time_step * change)
    return components


def plastic_return(c, plastic, cohesion):
    for _ in range(RETURN_ITERS):
        mean = (c[0] + c[1] + c[2]) / 3.0
        d = [c[0] - mean, c[1] - mean, c[2] - mean, c[3], c[4], c[5]]
        second = 0.5 * (d[0] * d[0] + d[1] * d[1] + d[2] * d[2])
        second = second + d[3] * d[3] + d[4] * d[4] + d[5] * d[5]
        tau = jnp.sqrt(second)
        limit = cohesion * (1.0 + plastic / (plastic + harden_scale))
        excess = jnp.maximum(tau + friction * 3.0 * mean - limit, 0.0)
        multiplier = (
            relax_rate * excess / (shear_mod + 9.0 * bulk_mod * friction * friction + harden_mod)
        )
        shrink = jnp.maximum(1.0 - shear_mod * multiplier / jnp.maximum(tau, tau_floor), 0.0)
        mean = mean - 3.0 * bulk_mod * friction * multiplier
        c = [
            d[0] * shrink + mean,
            d[1] * shrink + mean,
            d[2] * shrink + mean,
            d[3] * shrink,
            d[4] * shrink,
            d[5] * shrink,
        ]
        plastic = plastic + multiplier
    return c, plastic


def contact_rows(contact, flag, blocks):
    flag[...] = jnp.zeros_like(flag)
    for i in range(contact.shape[1]):
        flag[pl.ds(contact[0, i], 1), :] += 1.0
    return flag[0:blocks, :]


def rates_of(acc, own_acc, state, contact, flag):
    blocks, parts = state.shape[1:]
    contact_flag = contact_rows(contact, flag, blocks)
    x = [state[k] for k in range(3)]
    v = [state[k] for k in range(3, 6)]
    s = [state[k] for k in range(6, 12)]
    summed = [get_row(acc, k, blocks, ACC_PITCH) + get_row(own_acc, k, blocks, ACC_PITCH) for k in range(SOURCES)]
    return x, v, *section_rates(summed, x, v, s, contact_flag)


def half_kernel(
    pairs, total, lists, links, behind_depth, behind_strip, contact,
    right, far_src, far_left, terms, state, stress, plastic, cohesion,
    state_out,
    acc, own_acc, held, flag,
):
    sums(
        pairs, total, lists, links, (behind_depth, behind_strip),
        right, far_src, far_left, terms, acc, own_acc, held,
    )
    x, v, acceleration, strain = rates_of(acc, own_acc, state, contact, flag)
    components, _ = plastic_return(
        elastic_step([stress[c] for c in range(6)], strain, 0.5), plastic[...], cohesion[...]
    )
    inverse = state[15]
    rows = [x[k] + 0.5 * time_step * v[k] for k in range(3)]
    rows += [v[k] + 0.5 * time_step * acceleration[k] for k in range(3)]
    rows += [c * inverse for c in components]
    rows += [state[12], state[13], state[14], inverse]
    for k, row in enumerate(rows):
        state_out[k] = row


def end_kernel(
    pairs, total, lists, links, behind_depth, behind_strip, contact,
    right, far_src, far_left, terms, state, stress, plastic, cohesion, first,
    new_position, new_velocity, new_stress, new_plastic,
    acc, own_acc, held, flag,
):
    sums(
        pairs, total, lists, links, (behind_depth, behind_strip),
        right, far_src, far_left, terms, acc, own_acc, held,
    )
    _, half_v, acceleration, strain = rates_of(acc, own_acc, state, contact, flag)
    components, hardened = plastic_return(
        elastic_step([stress[c] for c in range(6)], strain, 1.0), plastic[...], cohesion[...]
    )
    live = state[14]
    for k in range(3):
        new_position[k] = (first[k] + time_step * half_v[k]) * live
        new_velocity[k] = (first[3 + k] + time_step * acceleration[k]) * live
    for c in range(6):
        new_stress[c] = components[c] * live
    new_plastic[...] = hardened * live


def shards(
    position, velocity, stress, plastic, particle_mass, density, cohesion,
    counts, block_pairs, pair_count, send_lists, cross_links, contact,
):
    position, velocity, stress = position[0, 0], velocity[0, 0], stress[0, 0]
    plastic, mass, density, cohesion = plastic[0, 0], particle_mass[0, 0], density[0, 0], cohesion[0, 0]
    counts, pairs, lists = counts[0], jnp.swapaxes(block_pairs[0, 0], 0, 1), send_lists[0, 0]
    links, contact = jnp.swapaxes(cross_links[0, 0], 1, 2), contact[0]
    blocks, parts = mass.shape
    rim = lists.shape[1]
    smem = pl.BlockSpec(memory_space=pltpu.SMEM)
    vmem = pl.BlockSpec(memory_space=pltpu.VMEM)
    hbm = pl.BlockSpec(memory_space=pltpu.MemorySpace.HBM)
    shape = jax.ShapeDtypeStruct
    i32 = jnp.int32

    def like(a):
        return shape(a.shape, a.dtype)

    state_shape = shape((STATE, blocks, parts), f32)
    count = pairs.shape[1]
    slots = (count + 2 * UNROLL - 1) // (2 * UNROLL) * (2 * UNROLL)
    ready = (
        shape((blocks + 1, FEATURES, parts), bf16),
        shape((4 * rim + 1, 2 * ROWS, parts), bf16),
        shape((4 * rim + 1, parts, FEATURES), bf16),
        shape((slots, 2, ROWS, parts), f32),
    )
    mass_shape = shape((4, 2, rim, parts), f32)
    behind_shape = shape((8, parts), i32)
    dma = pltpu.SemaphoreType.DMA

    def share_scratch(sent_rows):
        rims = pltpu.VMEM((4, rim * sent_rows, parts), f32)
        tiles = pltpu.VMEM((2 * UNROLL, parts, parts), bf16)
        tmp = pltpu.VMEM((max(blocks, rim) * PITCH, parts), f32)
        return [
            pltpu.VMEM((blocks, STATE, parts), f32), rims, rims,
            pltpu.VMEM((blocks + 1, 2 * ROWS, parts), bf16),
            pltpu.VMEM((blocks + 1, parts, FEATURES), bf16),
            tiles, tiles, tmp, tmp, tmp, dma((4,)), dma((4,)),
        ]

    acc = pltpu.VMEM(((blocks + 1) * ACC_PITCH, parts), f32)
    tile_scratch = [
        acc, acc,
        pltpu.VMEM((8 * FACE_UNROLL, parts, parts), bf16),
        pltpu.VMEM((blocks + 8, parts), f32),
    ]
    params = pltpu.CompilerParams(vmem_limit_bytes=24 << 20)

    state, *rest = pl.pallas_call(
        begin_kernel,
        out_shape=(state_shape,) + ready + (mass_shape, behind_shape, behind_shape)
        + tuple(like(a) for a in (stress, plastic, cohesion, lists, links, pairs, contact)),
        in_specs=[smem] + [hbm] * 12,
        out_specs=(vmem,) * 15,
        scratch_shapes=[pltpu.SMEM(a.shape, i32) for a in (counts, lists, links, pairs)]
        + [pltpu.VMEM((blocks, parts), f32)]
        + [pltpu.VMEM(a.shape, f32) for a in (position, velocity, mass, density)]
        + [pltpu.VMEM((2, 8, parts), i32)]
        + [dma((15,)), dma((2,)), dma((2,))]
        + share_scratch(LIVE_ROWS),
        compiler_params=pltpu.CompilerParams(
            vmem_limit_bytes=24 << 20, collective_id=0, has_side_effects=True
        ),
        name="begin",
    )(pair_count, *(
        pltpu.with_memory_space_constraint(a, pltpu.MemorySpace.HBM)
        for a in (counts, lists, links, pairs, contact, position, velocity, stress, mass, density, plastic, cohesion)
    ))
    prepared, far_mass, rest = rest[:4], rest[4], rest[5:]
    behind, (stress_v, plastic_v, cohesion_v, lists_v, links_v, pairs_v, contact_v) = rest[:2], rest[2:]
    ints = (pairs_v, pair_count, lists_v, links_v, *behind, contact_v)
    cost = pl.CostEstimate(flops=pairs.shape[1] * parts * parts * 1000, bytes_accessed=8 << 20, transcendentals=0)
    half = pl.pallas_call(
        half_kernel,
        out_shape=state_shape,
        in_specs=[smem] * 7 + [vmem] * 8,
        out_specs=vmem,
        scratch_shapes=tile_scratch,
        compiler_params=params,
        cost_estimate=cost,
        name="half_step",
    )(*ints, *prepared, state, stress_v, plastic_v, cohesion_v)
    prepared = pl.pallas_call(
        again_kernel,
        out_shape=ready,
        in_specs=[smem] * 3 + [vmem] * 2,
        out_specs=(vmem,) * 4,
        scratch_shapes=share_scratch(MOVING_ROWS),
        compiler_params=pltpu.CompilerParams(
            vmem_limit_bytes=24 << 20, collective_id=1, has_side_effects=True
        ),
        name="again",
    )(pair_count, lists_v, pairs_v, half, far_mass)
    outs = pl.pallas_call(
        end_kernel,
        out_shape=(
            shape(position.shape, f32), shape(velocity.shape, f32), shape(stress.shape, f32), shape(plastic.shape, f32)
        ),
        in_specs=[smem] * 7 + [vmem] * 9,
        out_specs=(vmem,) * 4,
        scratch_shapes=tile_scratch,
        compiler_params=params,
        cost_estimate=cost,
        name="full_step",
    )(*ints, *prepared, half, stress_v, plastic_v, cohesion_v, state)
    return tuple(out[None, None] for out in outs)


def solution(mesh):
    def spec(rank):
        return P("strip", "depth", *([None] * (rank - 2)))

    return jax.shard_map(
        shards,
        mesh=mesh,
        in_specs=tuple(spec(r) for r in (5, 5, 5, 4, 4, 4, 4, 3, 4, 2, 4, 5, 3)),
        out_specs=tuple(spec(r) for r in (5, 5, 5, 4)),
        check_vma=False,
    )
```

```python
import jax
import jax.numpy as jnp
from jax import lax
from jax.experimental import pallas as pl
from jax.experimental.pallas import tpu as pltpu
from jax.sharding import PartitionSpec as P

RETURN_ITERS = 4

smooth_len = 1.5
kernel_coef = -105.0 / (3.141592653589793 * 1.5**5)
time_step = 0.25
gravity = 1.0
spin_rate = 2.0
blade_stiff = 4.0
bulk_mod = 2.0
shear_mod = 1.5
friction = 0.25
harden_scale = 0.05
harden_mod = 0.5
relax_rate = 0.7
tau_floor = 0.5
voigt_index = ((0, 3, 5), (3, 1, 4), (5, 4, 2))
voigt_pairs = ((0, 0), (1, 1), (2, 2), (0, 1), (1, 2), (0, 2))

STATE = 16
SOURCES = 26
ROWS = 32
FEATURES = 32
DISTANCES = 24
UNROLL = 32
FACE_UNROLL = 8
PITCH = 36
LIVE_ROWS = 14
MOVING_ROWS = 9
ACC_PITCH = 40
MESH = pl.DeviceIdType.MESH
f32 = jnp.float32
bf16 = jnp.bfloat16


def source_rows(x, v, s, mass, volume):
    rows = [mass]
    rows += [mass * x[k] for k in range(3)]
    rows += [mass * s[c] for c in range(6)]
    for k in range(3):
        i = voigt_index[k]
        rows.append(mass * (s[i[0]] * x[0] + s[i[1]] * x[1] + s[i[2]] * x[2]))
    rows.append(volume)
    rows += [volume * v[k] for k in range(3)]
    rows += [volume * x[k] for k in range(3)]
    for a, b in voigt_pairs:
        rows.append(volume * (0.5 * (v[a] * x[b] + v[b] * x[a])))
    return rows


def split3(value):
    high = value.astype(bf16).astype(f32)
    rest = value - high
    mid = rest.astype(bf16).astype(f32)
    low = (rest - mid).astype(bf16).astype(f32)
    return high, mid, low


PRODUCTS = ((0, 0), (0, 1), (1, 0), (1, 1), (0, 2), (2, 0))


def distance_rows(x, row_side, col_side):
    scaled = [x[k] * (1.0 / smooth_len) for k in range(3)]
    parts = [split3(y) for y in scaled]
    norm = split3(scaled[0] * scaled[0] + scaled[1] * scaled[1] + scaled[2] * scaled[2])
    one = jnp.ones_like(x[0])
    left, right = [], []
    for k in range(3):
        for a, b in PRODUCTS:
            left.append(-2.0 * parts[k][a])
            right.append(parts[k][b])
    left += list(norm) + [one] * 3
    right += [one] * 3 + list(norm)
    return (left if row_side else None, right if col_side else None)


def put_rows(ref, rows, start, count, stride):
    for k, row in enumerate(rows):
        ref[pl.ds(start * stride + k, count, stride=stride), :] = row


def get_row(ref, k, count, stride):
    return ref[pl.ds(k, count, stride=stride), :]


def close_kernel(left, right):
    squared = lax.dot_general(left, right, (((1,), (0,)), ((), ())), preferred_element_type=f32)
    squared = jnp.maximum(squared, 1e-30)
    near = jnp.maximum(1.0 - squared * lax.rsqrt(squared), 0.0)
    return (near * near * near).astype(bf16)


def fold(result):
    return result[:ROWS] + result[ROWS:]


def spread(sources, kernel):
    return fold(
        lax.dot_general(sources, kernel, (((1,), (0,)), ((), ())), preferred_element_type=f32)
    )


def pipelined(steps, width, prepare, apply, finish, beside=None):
    for u in range(width):
        prepare(0, u, 0)

    def one(g, half, more):
        found = []
        for u in range(width):
            found += apply(g, u, half)
            if more:
                prepare(g + 1, u, 1 - half)
            if beside is not None:
                beside(g, u)
        finish(g, found)

    def step(i, carry):
        one(2 * i, 0, True)
        one(2 * i + 1, 1, True)
        return carry

    lax.fori_loop(0, steps - 1, step, 0)
    one(2 * steps - 2, 0, True)
    one(2 * steps - 1, 1, False)


def split_sources(tmp, b):
    rows = tmp[pl.ds(b * PITCH, ROWS), :]
    high = rows.astype(bf16)
    return high, (rows - high.astype(f32)).astype(bf16)


def store_features(tmps, src, right, left, start, count):
    def one(b, carry):
        high, low = split_sources(tmps[0], b)
        src[start + b, 0:ROWS, :] = high
        src[start + b, ROWS : 2 * ROWS, :] = low
        left[start + b] = tmps[1][pl.ds(b * PITCH, FEATURES), :].T.astype(bf16)
        if right is not None:
            right[start + b] = tmps[2][pl.ds(b * PITCH, FEATURES), :].astype(bf16)
        return carry

    lax.fori_loop(0, count, one, 0, unroll=16)


def gather_rims(rows, raw, lists, sends, after):
    for k, row in enumerate(rows):
        raw[:, k, :] = row
    width = len(rows)
    for face in range(4):
        for slot in range(lists.shape[1]):
            sends[face, slot * width : (slot + 1) * width, :] = raw[lists[face, slot]][:width]
        after(face)


class Faces:
    def __init__(self):
        d, n = lax.axis_index("depth"), lax.axis_size("depth")
        s, m = lax.axis_index("strip"), lax.axis_size("strip")
        self.there = (d < n - 1, d > 0, None, None)
        self.device = (
            {"depth": d + 1}, {"depth": d - 1},
            {"strip": lax.rem(s + 1, m)}, {"strip": lax.rem(s + m - 1, m)},
        )

    def when(self, face, act):
        if self.there[face] is None:
            act()
        else:
            pl.when(self.there[face])(act)

    def greet(self):
        barrier = pltpu.get_barrier_semaphore()
        for face in range(4):
            def act(face=face):
                pl.semaphore_signal(barrier, inc=1, device_id=self.device[face], device_id_type=MESH)
            self.when(face, act)

    def meet(self):
        peers = sum(1 if there is None else there.astype(jnp.int32) for there in self.there)
        pl.semaphore_wait(pltpu.get_barrier_semaphore(), peers)

    def copy(self, face, source, target, sent, got):
        return pltpu.make_async_remote_copy(
            src_ref=source, dst_ref=target, send_sem=sent, recv_sem=got,
            device_id=self.device[face], device_id_type=MESH,
        )


def prepare_local(rows, src, right, left, tmps, blocks):
    slots = tmps[0].shape[0] // PITCH
    zero = jnp.zeros((slots, rows[0].shape[1]), f32)
    for tmp, used in zip(tmps, (SOURCES, DISTANCES, DISTANCES)):
        for k in range(used, ROWS):
            tmp[pl.ds(k, slots, stride=PITCH), :] = zero
    sources = source_rows(rows[0:3], rows[3:6], rows[6:12], rows[12], rows[13])
    put_rows(tmps[0], sources, 0, blocks, PITCH)
    left_rows, right_rows = distance_rows(rows[0:3], True, True)
    put_rows(tmps[1], left_rows, 0, blocks, PITCH)
    put_rows(tmps[2], right_rows, 0, blocks, PITCH)
    store_features(tmps, src, right, left, 0, blocks)
    src[blocks] = jnp.zeros(src.shape[1:], bf16)
    right[blocks] = jnp.zeros(right.shape[1:], bf16)
    left[blocks] = jnp.zeros(left.shape[1:], bf16)


def prepare_far(got, start, src, left, tmps):
    count = got[0].shape[0]
    put_rows(tmps[0], source_rows(got[0:3], got[3:6], got[6:12], got[12], got[13]), 0, count, PITCH)
    put_rows(tmps[1], distance_rows(got[0:3], True, False)[0], 0, count, PITCH)
    store_features(tmps, src, None, left, start, count)


def pair_at(pairs, live, q, blocks):
    at = jnp.minimum(q, pairs.shape[1] - 1)
    a, b = pairs[0, at], pairs[1, at]
    return jnp.where(q < live, a, blocks), jnp.where(q < live, b, blocks)


def local_terms(pairs, total, src, right, left, terms, held, turned):
    blocks = src.shape[0] - 1
    live = total[0, 0]

    def prepare(g, u, slot):
        a, b = pair_at(pairs, live, g * UNROLL + u, blocks)
        kernel = close_kernel(left[a], right[b])
        held[slot * UNROLL + u] = kernel
        turned[slot * UNROLL + u] = kernel.T

    def apply(g, u, slot):
        q = g * UNROLL + u
        a, b = pair_at(pairs, live, q, blocks)
        at = slot * UNROLL + u
        return [(q, 0, spread(src[b], turned[at])), (q, 1, spread(src[a], held[at]))]

    def finish(g, found):
        for q, side, value in found:
            terms[q, side] = value

    pipelined(terms.shape[0] // (2 * UNROLL), UNROLL, prepare, apply, finish)


def share(
    faces, rows, first, far_kept, lists, pairs, total, raw, sends, far, sent, got,
    right, far_src, far_left, terms, src, left, held, turned, tmps, extra,
):
    blocks, rim = rows[0].shape[0], lists.shape[1]
    sent_rows = LIVE_ROWS if first else MOVING_ROWS
    copies = [
        faces.copy(face, sends.at[face], far.at[face ^ 1], sent.at[face], got.at[face ^ 1])
        for face in range(4)
    ]

    def after(face):
        if face == 0:
            faces.meet()
        faces.when(face, copies[face].start)

    gather_rims(rows[:LIVE_ROWS] if first else rows[3:12], raw, lists, sends, after)
    extra()
    prepare_local(rows, src, right, left, tmps, blocks)
    local_terms(pairs, total, src, right, left, terms, held, turned)
    far_src[4 * rim] = jnp.zeros(far_src.shape[1:], bf16)
    far_left[4 * rim] = jnp.zeros(far_left.shape[1:], bf16)
    for pair in ((2, 3), (0, 1)):
        halves = []
        for face in pair:
            if faces.there[face] is not None:
                @pl.when(jnp.logical_not(faces.there[face]))
                def _():
                    far[face] = jnp.zeros(far.shape[1:], f32)
            faces.when(face, copies[face ^ 1].wait_recv)
            halves.append([get_row(far.at[face], k, rim, sent_rows) for k in range(sent_rows)])
        arrived = [jnp.concatenate(rows, axis=0) for rows in zip(*halves)]
        kept = slice(pair[0] * rim, (pair[0] + 2) * rim)
        if first:
            far_kept[0, kept], far_kept[1, kept] = arrived[12], arrived[13]
            for k in range(3):
                far_kept[2 + k, kept] = arrived[k] + 0.5 * time_step * arrived[3 + k]
        else:
            arrived = [far_kept[2 + k, kept] for k in range(3)] + arrived
            arrived += [far_kept[0, kept], far_kept[1, kept]]
        prepare_far(arrived, pair[0] * rim, far_src, far_left, tmps)
    for face in range(4):
        faces.when(face, copies[face].wait_send)


def begin_kernel(
    total, counts_in, lists_in, links_in, pairs_in, contact_in, pos_in, vel_in, stress_in, mass_in, density_in,
    plastic_in, cohesion_in,
    state, right, far_src, far_left, terms, far_kept, behind_depth, behind_strip,
    stress, plastic, cohesion, lists_out, links_out, pairs_out, contact,
    counts, lists, links, pairs, occ, pos, vel, mass, density, packed,
    sems, pack_sent, pack_got,
    raw, sends, far, src, left, held, turned, tmp0, tmp1, tmp2, sent, got,
):
    faces = Faces()
    faces.greet()
    moved = (
        (counts_in, counts), (lists_in, lists), (pos_in, pos), (vel_in, vel), (stress_in, stress),
        (mass_in, mass), (density_in, density), (links_in, links),
        (plastic_in, plastic), (cohesion_in, cohesion),
        (lists_in, lists_out), (links_in, links_out), (pairs_in, pairs_out), (contact_in, contact),
        (pairs_in, pairs),
    )
    copies = [pltpu.make_async_copy(a, b, sems.at[i]) for i, (a, b) in enumerate(moved)]
    for copy in copies:
        copy.start()
    blocks, parts = mass.shape
    lane = lax.broadcasted_iota(jnp.int32, (1, parts), 1)
    packed[...] = jnp.zeros(packed.shape, jnp.int32)
    copies[0].wait()
    for b in range(blocks):
        occ[b : b + 1, :] = jnp.where(lane < counts[0, b], 1.0, 0.0)
    live = occ[...]
    for copy in copies[1:7] + copies[14:]:
        copy.wait()
    rho = density[...]
    inverse = 1.0 / (rho * rho)
    weighted = mass[...] * live * kernel_coef
    rows = [pos[k] for k in range(3)] + [vel[k] for k in range(3)]
    rows += [stress[c] * inverse for c in range(6)]
    rows += [weighted, weighted / rho, live, inverse]
    for k, row in enumerate(rows):
        state[k] = row
    packs = (
        faces.copy(0, packed.at[0], behind_depth, pack_sent.at[0], pack_got.at[0]),
        faces.copy(2, packed.at[1], behind_strip, pack_sent.at[1], pack_got.at[1]),
    )

    def extra():
        copies[7].wait()
        for face in range(2):
            for side in range(2):
                row = jnp.zeros((1, parts), jnp.int32)
                for q in range(links.shape[2]):
                    row = jnp.where(lane == q, links[face, side, q], row)
                packed[face, side : side + 1, :] = row
            faces.when(2 * face, packs[face].start)

    share(
        faces, rows, True, far_kept, lists, pairs, total, raw, sends, far, sent, got,
        right, far_src, far_left, terms, src, left, held, turned, (tmp0, tmp1, tmp2), extra,
    )

    @pl.when(jnp.logical_not(faces.there[1]))
    def _():
        behind_depth[...] = jnp.zeros(behind_depth.shape, jnp.int32)

    faces.when(1, packs[0].wait_recv)
    packs[1].wait_recv()
    faces.when(0, packs[0].wait_send)
    packs[1].wait_send()
    for copy in copies[8:14]:
        copy.wait()


def again_kernel(
    total, lists, pairs, state, far_kept, right, far_src, far_left, terms,
    raw, sends, far, src, left, held, turned, tmp0, tmp1, tmp2, sent, got,
):
    faces = Faces()
    faces.greet()
    rows = [state[k] for k in range(STATE)]
    share(
        faces, rows, False, far_kept, lists, pairs, total, raw, sends, far, sent, got,
        right, far_src, far_left, terms, src, left, held, turned, (tmp0, tmp1, tmp2),
        lambda: None,
    )


def add_block(acc, at, value):
    rows = pl.ds(pl.multiple_of(at * ACC_PITCH, 8), ROWS)
    acc[rows, :] += value


def sums(pairs, total, lists, links, links_behind, right, src, left, terms, acc, own_acc, held):
    acc[...] = jnp.zeros(acc.shape, f32)
    own_acc[...] = jnp.zeros(own_acc.shape, f32)
    rim = lists.shape[1]
    blocks = right.shape[0] - 1
    live = total[0, 0]
    cross = links.shape[2]
    whole = cross % (2 * FACE_UNROLL) == 0

    def entry(g, u):
        q = g * FACE_UNROLL + u // 4
        at = jnp.minimum(q, cross - 1)
        face, behind = (u % 4) // 2, u % 2
        if behind:
            own = lists[2 * face + 1, links_behind[face][1, at]]
            far_slot = links_behind[face][0, at]
        else:
            own, far_slot = lists[2 * face, links[face, 0, at]], links[face, 1, at]
        far_slot = (u % 4) * rim + far_slot
        return own, far_slot if whole else jnp.where(q < cross, far_slot, 4 * rim)

    width = 4 * FACE_UNROLL

    def prepare(g, u, slot):
        own, far_slot = entry(g, u)
        held[slot * width + u] = close_kernel(left[far_slot], right[own])

    def apply(g, u, slot):
        own, far_slot = entry(g, u)
        return [(own, spread(src[far_slot], held[slot * width + u]))]

    steps = (cross + 2 * FACE_UNROLL - 1) // (2 * FACE_UNROLL)
    count = pairs.shape[1]
    share_of = (count + 2 * steps - 1) // (2 * steps)
    assert share_of <= width

    def beside(g, u):
        if u < share_of:
            q = g * share_of + u
            a, b = pair_at(pairs, live, q, blocks)
            at = jnp.minimum(q, count - 1)
            add_block(own_acc, a, terms[at, 0])
            add_block(own_acc, jnp.where(a == b, blocks, b), terms[at, 1])

    def finish(g, found):
        for at, value in found:
            add_block(acc, at, value)

    pipelined(steps, width, prepare, apply, finish, beside)


def section_rates(summed, x, v, s, contact_flag):
    blade = (spin_rate * x[2], jnp.zeros_like(x[1]), -spin_rate * x[0])
    acceleration = []
    arm = [x[l] * summed[0] - summed[1 + l] for l in range(3)]
    for k in range(3):
        total = -summed[10 + k] + blade_stiff * contact_flag * (blade[k] - v[k])
        for l in range(3):
            slot = voigt_index[k][l]
            total = total + s[slot] * arm[l] + x[l] * summed[4 + slot]
        if k == 2:
            total = total - gravity
        acceleration.append(total)
    strain = []
    for c, (k, l) in enumerate(voigt_pairs):
        rate = 0.5 * (x[l] * summed[14 + k] + x[k] * summed[14 + l]) - summed[20 + c]
        rate = rate - 0.5 * summed[13] * (v[k] * x[l] + v[l] * x[k])
        rate = rate + 0.5 * (v[k] * summed[17 + l] + v[l] * summed[17 + k])
        strain.append(rate)
    return acceleration, strain


def elastic_step(stress, strain, fraction):
    volumetric = strain[0] + strain[1] + strain[2]
    lame_first = bulk_mod - 2.0 * shear_mod / 3.0
    components = []
    for c in range(6):
        change = 2.0 * shear_mod * strain[c]
        if c < 3:
            change = change + lame_first * volumetric
        components.append(stress[c] + fraction * time_step * change)
    return components


def plastic_return(c, plastic, cohesion):
    for _ in range(RETURN_ITERS):
        mean = (c[0] + c[1] + c[2]) / 3.0
        d = [c[0] - mean, c[1] - mean, c[2] - mean, c[3], c[4], c[5]]
        second = 0.5 * (d[0] * d[0] + d[1] * d[1] + d[2] * d[2])
        second = second + d[3] * d[3] + d[4] * d[4] + d[5] * d[5]
        tau = jnp.sqrt(second)
        limit = cohesion * (1.0 + plastic / (plastic + harden_scale))
        excess = jnp.maximum(tau + friction * 3.0 * mean - limit, 0.0)
        multiplier = (
            relax_rate * excess / (shear_mod + 9.0 * bulk_mod * friction * friction + harden_mod)
        )
        shrink = jnp.maximum(1.0 - shear_mod * multiplier / jnp.maximum(tau, tau_floor), 0.0)
        mean = mean - 3.0 * bulk_mod * friction * multiplier
        c = [
            d[0] * shrink + mean,
            d[1] * shrink + mean,
            d[2] * shrink + mean,
            d[3] * shrink,
            d[4] * shrink,
            d[5] * shrink,
        ]
        plastic = plastic + multiplier
    return c, plastic


def contact_rows(contact, flag, blocks):
    flag[...] = jnp.zeros_like(flag)
    for i in range(contact.shape[1]):
        flag[pl.ds(contact[0, i], 1), :] += 1.0
    return flag[0:blocks, :]


def rates_of(acc, own_acc, state, contact, flag):
    blocks, parts = state.shape[1:]
    contact_flag = contact_rows(contact, flag, blocks)
    x = [state[k] for k in range(3)]
    v = [state[k] for k in range(3, 6)]
    s = [state[k] for k in range(6, 12)]
    summed = [get_row(acc, k, blocks, ACC_PITCH) + get_row(own_acc, k, blocks, ACC_PITCH) for k in range(SOURCES)]
    return x, v, *section_rates(summed, x, v, s, contact_flag)


def half_kernel(
    pairs, total, lists, links, behind_depth, behind_strip, contact,
    right, far_src, far_left, terms, state, stress, plastic, cohesion,
    state_out,
    acc, own_acc, held, flag,
):
    sums(
        pairs, total, lists, links, (behind_depth, behind_strip),
        right, far_src, far_left, terms, acc, own_acc, held,
    )
    x, v, acceleration, strain = rates_of(acc, own_acc, state, contact, flag)
    components, _ = plastic_return(
        elastic_step([stress[c] for c in range(6)], strain, 0.5), plastic[...], cohesion[...]
    )
    inverse = state[15]
    rows = [x[k] + 0.5 * time_step * v[k] for k in range(3)]
    rows += [v[k] + 0.5 * time_step * acceleration[k] for k in range(3)]
    rows += [c * inverse for c in components]
    rows += [state[12], state[13], state[14], inverse]
    for k, row in enumerate(rows):
        state_out[k] = row


def end_kernel(
    pairs, total, lists, links, behind_depth, behind_strip, contact,
    right, far_src, far_left, terms, state, stress, plastic, cohesion, first,
    new_position, new_velocity, new_stress, new_plastic,
    acc, own_acc, held, flag,
):
    sums(
        pairs, total, lists, links, (behind_depth, behind_strip),
        right, far_src, far_left, terms, acc, own_acc, held,
    )
    _, half_v, acceleration, strain = rates_of(acc, own_acc, state, contact, flag)
    components, hardened = plastic_return(
        elastic_step([stress[c] for c in range(6)], strain, 1.0), plastic[...], cohesion[...]
    )
    live = state[14]
    for k in range(3):
        new_position[k] = (first[k] + time_step * half_v[k]) * live
        new_velocity[k] = (first[3 + k] + time_step * acceleration[k]) * live
    for c in range(6):
        new_stress[c] = components[c] * live
    new_plastic[...] = hardened * live


def shards(
    position, velocity, stress, plastic, particle_mass, density, cohesion,
    counts, block_pairs, pair_count, send_lists, cross_links, contact,
):
    position, velocity, stress = position[0, 0], velocity[0, 0], stress[0, 0]
    plastic, mass, density, cohesion = plastic[0, 0], particle_mass[0, 0], density[0, 0], cohesion[0, 0]
    counts, pairs, lists = counts[0], jnp.swapaxes(block_pairs[0, 0], 0, 1), send_lists[0, 0]
    links, contact = jnp.swapaxes(cross_links[0, 0], 1, 2), contact[0]
    blocks, parts = mass.shape
    rim = lists.shape[1]
    smem = pl.BlockSpec(memory_space=pltpu.SMEM)
    vmem = pl.BlockSpec(memory_space=pltpu.VMEM)
    hbm = pl.BlockSpec(memory_space=pltpu.MemorySpace.HBM)
    shape = jax.ShapeDtypeStruct
    i32 = jnp.int32

    def like(a):
        return shape(a.shape, a.dtype)

    state_shape = shape((STATE, blocks, parts), f32)
    count = pairs.shape[1]
    slots = (count + 2 * UNROLL - 1) // (2 * UNROLL) * (2 * UNROLL)
    ready = (
        shape((blocks + 1, FEATURES, parts), bf16),
        shape((4 * rim + 1, 2 * ROWS, parts), bf16),
        shape((4 * rim + 1, parts, FEATURES), bf16),
        shape((slots, 2, ROWS, parts), f32),
    )
    kept_shape = shape((5, 4 * rim, parts), f32)
    behind_shape = shape((8, parts), i32)
    dma = pltpu.SemaphoreType.DMA

    def share_scratch(sent_rows):
        rims = pltpu.VMEM((4, rim * sent_rows, parts), f32)
        tiles = pltpu.VMEM((2 * UNROLL, parts, parts), bf16)
        tmp = pltpu.VMEM((max(blocks, 2 * rim) * PITCH, parts), f32)
        return [
            pltpu.VMEM((blocks, STATE, parts), f32), rims, rims,
            pltpu.VMEM((blocks + 1, 2 * ROWS, parts), bf16),
            pltpu.VMEM((blocks + 1, parts, FEATURES), bf16),
            tiles, tiles, tmp, tmp, tmp, dma((4,)), dma((4,)),
        ]

    acc = pltpu.VMEM(((blocks + 1) * ACC_PITCH, parts), f32)
    tile_scratch = [
        acc, acc,
        pltpu.VMEM((8 * FACE_UNROLL, parts, parts), bf16),
        pltpu.VMEM((blocks + 8, parts), f32),
    ]
    params = pltpu.CompilerParams(vmem_limit_bytes=24 << 20)

    state, *rest = pl.pallas_call(
        begin_kernel,
        out_shape=(state_shape,) + ready + (kept_shape, behind_shape, behind_shape)
        + tuple(like(a) for a in (stress, plastic, cohesion, lists, links, pairs, contact)),
        in_specs=[smem] + [hbm] * 12,
        out_specs=(vmem,) * 15,
        scratch_shapes=[pltpu.SMEM(a.shape, i32) for a in (counts, lists, links, pairs)]
        + [pltpu.VMEM((blocks, parts), f32)]
        + [pltpu.VMEM(a.shape, f32) for a in (position, velocity, mass, density)]
        + [pltpu.VMEM((2, 8, parts), i32)]
        + [dma((15,)), dma((2,)), dma((2,))]
        + share_scratch(LIVE_ROWS),
        compiler_params=pltpu.CompilerParams(
            vmem_limit_bytes=24 << 20, collective_id=0, has_side_effects=True
        ),
        name="begin",
    )(pair_count, *(
        pltpu.with_memory_space_constraint(a, pltpu.MemorySpace.HBM)
        for a in (counts, lists, links, pairs, contact, position, velocity, stress, mass, density, plastic, cohesion)
    ))
    prepared, far_kept, rest = rest[:4], rest[4], rest[5:]
    behind, (stress_v, plastic_v, cohesion_v, lists_v, links_v, pairs_v, contact_v) = rest[:2], rest[2:]
    ints = (pairs_v, pair_count, lists_v, links_v, *behind, contact_v)
    cost = pl.CostEstimate(flops=pairs.shape[1] * parts * parts * 1000, bytes_accessed=8 << 20, transcendentals=0)
    half = pl.pallas_call(
        half_kernel,
        out_shape=state_shape,
        in_specs=[smem] * 7 + [vmem] * 8,
        out_specs=vmem,
        scratch_shapes=tile_scratch,
        compiler_params=params,
        cost_estimate=cost,
        name="half_step",
    )(*ints, *prepared, state, stress_v, plastic_v, cohesion_v)
    prepared = pl.pallas_call(
        again_kernel,
        out_shape=ready,
        in_specs=[smem] * 3 + [vmem] * 2,
        out_specs=(vmem,) * 4,
        scratch_shapes=share_scratch(MOVING_ROWS),
        compiler_params=pltpu.CompilerParams(
            vmem_limit_bytes=24 << 20, collective_id=1, has_side_effects=True
        ),
        name="again",
    )(pair_count, lists_v, pairs_v, half, far_kept)
    outs = pl.pallas_call(
        end_kernel,
        out_shape=(
            shape(position.shape, f32), shape(velocity.shape, f32), shape(stress.shape, f32), shape(plastic.shape, f32)
        ),
        in_specs=[smem] * 7 + [vmem] * 9,
        out_specs=(vmem,) * 4,
        scratch_shapes=tile_scratch,
        compiler_params=params,
        cost_estimate=cost,
        name="full_step",
    )(*ints, *prepared, half, stress_v, plastic_v, cohesion_v, state)
    return tuple(out[None, None] for out in outs)


def solution(mesh):
    def spec(rank):
        return P("strip", "depth", *([None] * (rank - 2)))

    return jax.shard_map(
        shards,
        mesh=mesh,
        in_specs=tuple(spec(r) for r in (5, 5, 5, 4, 4, 4, 4, 3, 4, 2, 4, 5, 3)),
        out_specs=tuple(spec(r) for r in (5, 5, 5, 4)),
        check_vma=False,
    )
```

```python
import jax
import jax.numpy as jnp
from jax import lax
from jax.experimental import pallas as pl
from jax.experimental.pallas import tpu as pltpu
from jax.sharding import PartitionSpec as P

RETURN_ITERS = 4

smooth_len = 1.5
kernel_coef = -105.0 / (3.141592653589793 * 1.5**5)
time_step = 0.25
gravity = 1.0
spin_rate = 2.0
blade_stiff = 4.0
bulk_mod = 2.0
shear_mod = 1.5
friction = 0.25
harden_scale = 0.05
harden_mod = 0.5
relax_rate = 0.7
tau_floor = 0.5
voigt_index = ((0, 3, 5), (3, 1, 4), (5, 4, 2))
voigt_pairs = ((0, 0), (1, 1), (2, 2), (0, 1), (1, 2), (0, 2))

STATE = 16
SOURCES = 26
ROWS = 32
FEATURES = 32
DISTANCES = 24
UNROLL = 32
FACE_UNROLL = 8
PITCH = 36
LIVE_ROWS = 14
MOVING_ROWS = 9
ACC_PITCH = 40
MESH = pl.DeviceIdType.MESH
f32 = jnp.float32
bf16 = jnp.bfloat16


def source_rows(x, v, s, mass, volume):
    rows = [mass]
    rows += [mass * x[k] for k in range(3)]
    rows += [mass * s[c] for c in range(6)]
    for k in range(3):
        i = voigt_index[k]
        rows.append(mass * (s[i[0]] * x[0] + s[i[1]] * x[1] + s[i[2]] * x[2]))
    rows.append(volume)
    rows += [volume * v[k] for k in range(3)]
    rows += [volume * x[k] for k in range(3)]
    for a, b in voigt_pairs:
        rows.append(volume * (0.5 * (v[a] * x[b] + v[b] * x[a])))
    return rows


def split3(value):
    high = value.astype(bf16).astype(f32)
    rest = value - high
    mid = rest.astype(bf16).astype(f32)
    low = (rest - mid).astype(bf16).astype(f32)
    return high, mid, low


PRODUCTS = ((0, 0), (0, 1), (1, 0), (1, 1), (0, 2), (2, 0))


def distance_rows(x, row_side, col_side):
    scaled = [x[k] * (1.0 / smooth_len) for k in range(3)]
    parts = [split3(y) for y in scaled]
    norm = split3(scaled[0] * scaled[0] + scaled[1] * scaled[1] + scaled[2] * scaled[2])
    one = jnp.ones_like(x[0])
    left, right = [], []
    for k in range(3):
        for a, b in PRODUCTS:
            left.append(-2.0 * parts[k][a])
            right.append(parts[k][b])
    left += list(norm) + [one] * 3
    right += [one] * 3 + list(norm)
    return (left if row_side else None, right if col_side else None)


def put_rows(ref, rows, start, count, stride):
    for k, row in enumerate(rows):
        ref[pl.ds(start * stride + k, count, stride=stride), :] = row


def get_row(ref, k, count, stride):
    return ref[pl.ds(k, count, stride=stride), :]


def close_kernel(left, right):
    squared = lax.dot_general(left, right, (((1,), (0,)), ((), ())), preferred_element_type=f32)
    squared = jnp.maximum(squared, 1e-30)
    near = jnp.maximum(1.0 - squared * lax.rsqrt(squared), 0.0)
    return (near * near * near).astype(bf16)


def spread(sources, kernel):
    both = jnp.concatenate([sources[:ROWS], sources[ROWS:]], axis=1)
    twice = jnp.concatenate([kernel, kernel], axis=0)
    return lax.dot_general(both, twice, (((1,), (0,)), ((), ())), preferred_element_type=f32)


def pipelined(steps, width, prepare, apply, finish, beside=None, late=(None, None)):
    for u in range(width):
        prepare(0, u, 0)

    def one(g, half, more):
        found = []
        for u in range(width):
            found += apply(g, u, half)
            if more:
                prepare(g + 1, u, 1 - half)
            if beside is not None:
                beside(g, u)
        finish(g, found)

    def step(i, carry):
        one(2 * i, 0, True)
        one(2 * i + 1, 1, True)
        return carry

    lax.fori_loop(0, steps - 1, step, 0)
    for half in range(2):
        if late[half] is not None:
            late[half]()
        one(2 * steps - 2 + half, half, half == 0)


def split_sources(tmp, b):
    rows = tmp[pl.ds(b * PITCH, ROWS), :]
    high = rows.astype(bf16)
    return high, (rows - high.astype(f32)).astype(bf16)


def store_features(tmps, src, right, left, start, count):
    def one(b, carry):
        high, low = split_sources(tmps[0], b)
        src[start + b, 0:ROWS, :] = high
        src[start + b, ROWS : 2 * ROWS, :] = low
        left[start + b] = tmps[1][pl.ds(b * PITCH, FEATURES), :].T.astype(bf16)
        if right is not None:
            right[start + b] = tmps[2][pl.ds(b * PITCH, FEATURES), :].astype(bf16)
        return carry

    if right is None:
        for b in range(count):
            one(b, 0)
    else:
        lax.fori_loop(0, count, one, 0, unroll=16)


def gather_rims(rows, raw, lists, sends, after):
    for k, row in enumerate(rows):
        raw[:, k, :] = row
    width = len(rows)
    for face in range(4):
        for slot in range(lists.shape[1]):
            sends[face, slot * width : (slot + 1) * width, :] = raw[lists[face, slot]][:width]
        after(face)


class Faces:
    def __init__(self):
        d, n = lax.axis_index("depth"), lax.axis_size("depth")
        s, m = lax.axis_index("strip"), lax.axis_size("strip")
        self.there = (d < n - 1, d > 0, None, None)
        self.device = (
            {"depth": d + 1}, {"depth": d - 1},
            {"strip": lax.rem(s + 1, m)}, {"strip": lax.rem(s + m - 1, m)},
        )

    def when(self, face, act):
        if self.there[face] is None:
            act()
        else:
            pl.when(self.there[face])(act)

    def greet(self):
        barrier = pltpu.get_barrier_semaphore()
        for face in range(4):
            def act(face=face):
                pl.semaphore_signal(barrier, inc=1, device_id=self.device[face], device_id_type=MESH)
            self.when(face, act)

    def meet(self):
        peers = sum(1 if there is None else there.astype(jnp.int32) for there in self.there)
        pl.semaphore_wait(pltpu.get_barrier_semaphore(), peers)

    def copy(self, face, source, target, sent, got):
        return pltpu.make_async_remote_copy(
            src_ref=source, dst_ref=target, send_sem=sent, recv_sem=got,
            device_id=self.device[face], device_id_type=MESH,
        )


def prepare_local(rows, src, right, left, tmps, blocks):
    slots = tmps[0].shape[0] // PITCH
    zero = jnp.zeros((slots, rows[0].shape[1]), f32)
    for tmp, used in zip(tmps, (SOURCES, DISTANCES, DISTANCES)):
        for k in range(used, ROWS):
            tmp[pl.ds(k, slots, stride=PITCH), :] = zero
    sources = source_rows(rows[0:3], rows[3:6], rows[6:12], rows[12], rows[13])
    put_rows(tmps[0], sources, 0, blocks, PITCH)
    left_rows, right_rows = distance_rows(rows[0:3], True, True)
    put_rows(tmps[1], left_rows, 0, blocks, PITCH)
    put_rows(tmps[2], right_rows, 0, blocks, PITCH)
    store_features(tmps, src, right, left, 0, blocks)
    src[blocks] = jnp.zeros(src.shape[1:], bf16)
    right[blocks] = jnp.zeros(right.shape[1:], bf16)
    left[blocks] = jnp.zeros(left.shape[1:], bf16)


def prepare_far(got, start, src, left, tmps):
    count = got[0].shape[0]
    put_rows(tmps[0], source_rows(got[0:3], got[3:6], got[6:12], got[12], got[13]), 0, count, PITCH)
    put_rows(tmps[1], distance_rows(got[0:3], True, False)[0], 0, count, PITCH)
    store_features(tmps, src, None, left, start, count)


def pair_at(pairs, live, q, blocks):
    at = jnp.minimum(q, pairs.shape[1] - 1)
    a, b = pairs[0, at], pairs[1, at]
    return jnp.where(q < live, a, blocks), jnp.where(q < live, b, blocks)


def local_terms(pairs, total, src, right, left, terms, held, turned, late):
    blocks = src.shape[0] - 1
    live = total[0, 0]

    def prepare(g, u, slot):
        a, b = pair_at(pairs, live, g * UNROLL + u, blocks)
        kernel = close_kernel(left[a], right[b])
        held[slot * UNROLL + u] = kernel
        turned[slot * UNROLL + u] = kernel.T

    def apply(g, u, slot):
        q = g * UNROLL + u
        a, b = pair_at(pairs, live, q, blocks)
        at = slot * UNROLL + u
        return [(q, 0, spread(src[b], turned[at])), (q, 1, spread(src[a], held[at]))]

    def finish(g, found):
        for q, side, value in found:
            terms[q, side] = value

    pipelined(terms.shape[0] // (2 * UNROLL), UNROLL, prepare, apply, finish, late=late)


def share(
    faces, rows, first, far_kept, lists, pairs, total, raw, sends, far, sent, got,
    right, far_src, far_left, terms, src, left, held, turned, tmps, extra,
):
    blocks, rim = rows[0].shape[0], lists.shape[1]
    sent_rows = LIVE_ROWS if first else MOVING_ROWS
    copies = [
        faces.copy(face, sends.at[face], far.at[face ^ 1], sent.at[face], got.at[face ^ 1])
        for face in range(4)
    ]

    def after(face):
        if face == 0:
            faces.meet()
        faces.when(face, copies[face].start)

    gather_rims(rows[:LIVE_ROWS] if first else rows[3:12], raw, lists, sends, after)
    extra()
    prepare_local(rows, src, right, left, tmps, blocks)
    far_src[4 * rim] = jnp.zeros(far_src.shape[1:], bf16)
    far_left[4 * rim] = jnp.zeros(far_left.shape[1:], bf16)

    def arrivals(pair):
        for face in pair:
            if faces.there[face] is not None:
                @pl.when(jnp.logical_not(faces.there[face]))
                def _():
                    far[face] = jnp.zeros(far.shape[1:], f32)
            faces.when(face, copies[face ^ 1].wait_recv)
        halves = [[get_row(far.at[face], k, rim, sent_rows) for k in range(sent_rows)] for face in pair]
        arrived = [jnp.concatenate(rows, axis=0) for rows in zip(*halves)]
        kept = slice(pair[0] * rim, (pair[0] + 2) * rim)
        if first:
            far_kept[0, kept], far_kept[1, kept] = arrived[12], arrived[13]
            for k in range(3):
                far_kept[2 + k, kept] = arrived[k] + 0.5 * time_step * arrived[3 + k]
        else:
            arrived = [far_kept[2 + k, kept] for k in range(3)] + arrived
            arrived += [far_kept[0, kept], far_kept[1, kept]]
        prepare_far(arrived, pair[0] * rim, far_src, far_left, tmps)

    strip, depth = (lambda: arrivals((2, 3))), (lambda: arrivals((0, 1)))
    late = (None, strip)
    local_terms(pairs, total, src, right, left, terms, held, turned, late)
    depth()
    for face in range(4):
        faces.when(face, copies[face].wait_send)


def begin_kernel(
    total, counts_in, lists_in, links_in, pairs_in, contact_in, pos_in, vel_in, stress_in, mass_in, density_in,
    plastic_in, cohesion_in,
    state, right, far_src, far_left, terms, far_kept, behind_depth, behind_strip,
    stress, plastic, cohesion, lists_out, links_out, pairs_out, contact,
    counts, lists, links, pairs, occ, pos, vel, mass, density, packed,
    sems, pack_sent, pack_got,
    raw, sends, far, src, left, held, turned, tmp0, tmp1, tmp2, sent, got,
):
    faces = Faces()
    faces.greet()
    moved = (
        (counts_in, counts), (lists_in, lists), (pos_in, pos), (vel_in, vel), (stress_in, stress),
        (mass_in, mass), (density_in, density), (links_in, links),
        (plastic_in, plastic), (cohesion_in, cohesion),
        (lists_in, lists_out), (links_in, links_out), (pairs_in, pairs_out), (contact_in, contact),
        (pairs_in, pairs),
    )
    copies = [pltpu.make_async_copy(a, b, sems.at[i]) for i, (a, b) in enumerate(moved)]
    for copy in copies:
        copy.start()
    blocks, parts = mass.shape
    lane = lax.broadcasted_iota(jnp.int32, (1, parts), 1)
    packed[...] = jnp.zeros(packed.shape, jnp.int32)
    copies[0].wait()
    for b in range(blocks):
        occ[b : b + 1, :] = jnp.where(lane < counts[0, b], 1.0, 0.0)
    live = occ[...]
    for copy in copies[1:7] + copies[14:]:
        copy.wait()
    rho = density[...]
    inverse = 1.0 / (rho * rho)
    weighted = mass[...] * live * kernel_coef
    rows = [pos[k] for k in range(3)] + [vel[k] for k in range(3)]
    rows += [stress[c] * inverse for c in range(6)]
    rows += [weighted, weighted / rho, live, inverse]
    for k, row in enumerate(rows):
        state[k] = row
    packs = (
        faces.copy(0, packed.at[0], behind_depth, pack_sent.at[0], pack_got.at[0]),
        faces.copy(2, packed.at[1], behind_strip, pack_sent.at[1], pack_got.at[1]),
    )

    def extra():
        copies[7].wait()
        for face in range(2):
            for side in range(2):
                row = jnp.zeros((1, parts), jnp.int32)
                for q in range(links.shape[2]):
                    row = jnp.where(lane == q, links[face, side, q], row)
                packed[face, side : side + 1, :] = row
            faces.when(2 * face, packs[face].start)

    share(
        faces, rows, True, far_kept, lists, pairs, total, raw, sends, far, sent, got,
        right, far_src, far_left, terms, src, left, held, turned, (tmp0, tmp1, tmp2), extra,
    )

    @pl.when(jnp.logical_not(faces.there[1]))
    def _():
        behind_depth[...] = jnp.zeros(behind_depth.shape, jnp.int32)

    faces.when(1, packs[0].wait_recv)
    packs[1].wait_recv()
    faces.when(0, packs[0].wait_send)
    packs[1].wait_send()
    for copy in copies[8:14]:
        copy.wait()


def again_kernel(
    total, lists, pairs, state, far_kept, right, far_src, far_left, terms,
    raw, sends, far, src, left, held, turned, tmp0, tmp1, tmp2, sent, got,
):
    faces = Faces()
    faces.greet()
    rows = [state[k] for k in range(STATE)]
    share(
        faces, rows, False, far_kept, lists, pairs, total, raw, sends, far, sent, got,
        right, far_src, far_left, terms, src, left, held, turned, (tmp0, tmp1, tmp2),
        lambda: None,
    )


def add_block(acc, at, value):
    rows = pl.ds(pl.multiple_of(at * ACC_PITCH, 8), ROWS)
    acc[rows, :] += value


def sums(pairs, total, lists, links, links_behind, right, src, left, terms, acc, own_acc, held):
    acc[...] = jnp.zeros(acc.shape, f32)
    own_acc[...] = jnp.zeros(own_acc.shape, f32)
    rim = lists.shape[1]
    blocks = right.shape[0] - 1
    live = total[0, 0]
    cross = links.shape[2]
    whole = cross % (2 * FACE_UNROLL) == 0

    def entry(g, u):
        q = g * FACE_UNROLL + u // 4
        at = jnp.minimum(q, cross - 1)
        face, behind = (u % 4) // 2, u % 2
        if behind:
            own = lists[2 * face + 1, links_behind[face][1, at]]
            far_slot = links_behind[face][0, at]
        else:
            own, far_slot = lists[2 * face, links[face, 0, at]], links[face, 1, at]
        far_slot = (u % 4) * rim + far_slot
        return own, far_slot if whole else jnp.where(q < cross, far_slot, 4 * rim)

    width = 4 * FACE_UNROLL

    def prepare(g, u, slot):
        own, far_slot = entry(g, u)
        held[slot * width + u] = close_kernel(left[far_slot], right[own])

    def apply(g, u, slot):
        own, far_slot = entry(g, u)
        return [(own, spread(src[far_slot], held[slot * width + u]))]

    steps = (cross + 2 * FACE_UNROLL - 1) // (2 * FACE_UNROLL)
    count = pairs.shape[1]
    share_of = (count + 2 * steps - 1) // (2 * steps)
    assert share_of <= width

    def beside(g, u):
        if u < share_of:
            q = g * share_of + u
            a, b = pair_at(pairs, live, q, blocks)
            at = jnp.minimum(q, count - 1)
            add_block(own_acc, a, terms[at, 0])
            add_block(own_acc, jnp.where(a == b, blocks, b), terms[at, 1])

    def finish(g, found):
        for at, value in found:
            add_block(acc, at, value)

    pipelined(steps, width, prepare, apply, finish, beside)


def section_rates(summed, x, v, s, contact_flag):
    blade = (spin_rate * x[2], jnp.zeros_like(x[1]), -spin_rate * x[0])
    acceleration = []
    arm = [x[l] * summed[0] - summed[1 + l] for l in range(3)]
    for k in range(3):
        total = -summed[10 + k] + blade_stiff * contact_flag * (blade[k] - v[k])
        for l in range(3):
            slot = voigt_index[k][l]
            total = total + s[slot] * arm[l] + x[l] * summed[4 + slot]
        if k == 2:
            total = total - gravity
        acceleration.append(total)
    strain = []
    for c, (k, l) in enumerate(voigt_pairs):
        rate = 0.5 * (x[l] * summed[14 + k] + x[k] * summed[14 + l]) - summed[20 + c]
        rate = rate - 0.5 * summed[13] * (v[k] * x[l] + v[l] * x[k])
        rate = rate + 0.5 * (v[k] * summed[17 + l] + v[l] * summed[17 + k])
        strain.append(rate)
    return acceleration, strain


def elastic_step(stress, strain, fraction):
    volumetric = strain[0] + strain[1] + strain[2]
    lame_first = bulk_mod - 2.0 * shear_mod / 3.0
    components = []
    for c in range(6):
        change = 2.0 * shear_mod * strain[c]
        if c < 3:
            change = change + lame_first * volumetric
        components.append(stress[c] + fraction * time_step * change)
    return components


def plastic_return(c, plastic, cohesion):
    for _ in range(RETURN_ITERS):
        mean = (c[0] + c[1] + c[2]) / 3.0
        d = [c[0] - mean, c[1] - mean, c[2] - mean, c[3], c[4], c[5]]
        second = 0.5 * (d[0] * d[0] + d[1] * d[1] + d[2] * d[2])
        second = second + d[3] * d[3] + d[4] * d[4] + d[5] * d[5]
        tau = jnp.sqrt(second)
        limit = cohesion * (1.0 + plastic / (plastic + harden_scale))
        excess = jnp.maximum(tau + friction * 3.0 * mean - limit, 0.0)
        multiplier = (
            relax_rate * excess / (shear_mod + 9.0 * bulk_mod * friction * friction + harden_mod)
        )
        shrink = jnp.maximum(1.0 - shear_mod * multiplier / jnp.maximum(tau, tau_floor), 0.0)
        mean = mean - 3.0 * bulk_mod * friction * multiplier
        c = [
            d[0] * shrink + mean,
            d[1] * shrink + mean,
            d[2] * shrink + mean,
            d[3] * shrink,
            d[4] * shrink,
            d[5] * shrink,
        ]
        plastic = plastic + multiplier
    return c, plastic


def contact_rows(contact, flag, blocks):
    flag[...] = jnp.zeros_like(flag)
    for i in range(contact.shape[1]):
        flag[pl.ds(contact[0, i], 1), :] += 1.0
    return flag[0:blocks, :]


def rates_of(acc, own_acc, state, contact, flag):
    blocks, parts = state.shape[1:]
    contact_flag = contact_rows(contact, flag, blocks)
    x = [state[k] for k in range(3)]
    v = [state[k] for k in range(3, 6)]
    s = [state[k] for k in range(6, 12)]
    summed = [get_row(acc, k, blocks, ACC_PITCH) + get_row(own_acc, k, blocks, ACC_PITCH) for k in range(SOURCES)]
    return x, v, *section_rates(summed, x, v, s, contact_flag)


def half_kernel(
    pairs, total, lists, links, behind_depth, behind_strip, contact,
    right, far_src, far_left, terms, state, stress, plastic, cohesion,
    state_out,
    acc, own_acc, held, flag,
):
    sums(
        pairs, total, lists, links, (behind_depth, behind_strip),
        right, far_src, far_left, terms, acc, own_acc, held,
    )
    x, v, acceleration, strain = rates_of(acc, own_acc, state, contact, flag)
    components, _ = plastic_return(
        elastic_step([stress[c] for c in range(6)], strain, 0.5), plastic[...], cohesion[...]
    )
    inverse = state[15]
    rows = [x[k] + 0.5 * time_step * v[k] for k in range(3)]
    rows += [v[k] + 0.5 * time_step * acceleration[k] for k in range(3)]
    rows += [c * inverse for c in components]
    rows += [state[12], state[13], state[14], inverse]
    for k, row in enumerate(rows):
        state_out[k] = row


def end_kernel(
    pairs, total, lists, links, behind_depth, behind_strip, contact,
    right, far_src, far_left, terms, state, stress, plastic, cohesion, first,
    new_position, new_velocity, new_stress, new_plastic,
    acc, own_acc, held, flag,
):
    sums(
        pairs, total, lists, links, (behind_depth, behind_strip),
        right, far_src, far_left, terms, acc, own_acc, held,
    )
    _, half_v, acceleration, strain = rates_of(acc, own_acc, state, contact, flag)
    components, hardened = plastic_return(
        elastic_step([stress[c] for c in range(6)], strain, 1.0), plastic[...], cohesion[...]
    )
    live = state[14]
    for k in range(3):
        new_position[k] = (first[k] + time_step * half_v[k]) * live
        new_velocity[k] = (first[3 + k] + time_step * acceleration[k]) * live
    for c in range(6):
        new_stress[c] = components[c] * live
    new_plastic[...] = hardened * live


def shards(
    position, velocity, stress, plastic, particle_mass, density, cohesion,
    counts, block_pairs, pair_count, send_lists, cross_links, contact,
):
    position, velocity, stress = position[0, 0], velocity[0, 0], stress[0, 0]
    plastic, mass, density, cohesion = plastic[0, 0], particle_mass[0, 0], density[0, 0], cohesion[0, 0]
    counts, pairs, lists = counts[0], jnp.swapaxes(block_pairs[0, 0], 0, 1), send_lists[0, 0]
    links, contact = jnp.swapaxes(cross_links[0, 0], 1, 2), contact[0]
    blocks, parts = mass.shape
    rim = lists.shape[1]
    smem = pl.BlockSpec(memory_space=pltpu.SMEM)
    vmem = pl.BlockSpec(memory_space=pltpu.VMEM)
    hbm = pl.BlockSpec(memory_space=pltpu.MemorySpace.HBM)
    shape = jax.ShapeDtypeStruct
    i32 = jnp.int32

    def like(a):
        return shape(a.shape, a.dtype)

    state_shape = shape((STATE, blocks, parts), f32)
    count = pairs.shape[1]
    slots = (count + 2 * UNROLL - 1) // (2 * UNROLL) * (2 * UNROLL)
    ready = (
        shape((blocks + 1, FEATURES, parts), bf16),
        shape((4 * rim + 1, 2 * ROWS, parts), bf16),
        shape((4 * rim + 1, parts, FEATURES), bf16),
        shape((slots, 2, ROWS, parts), f32),
    )
    kept_shape = shape((5, 4 * rim, parts), f32)
    behind_shape = shape((8, parts), i32)
    dma = pltpu.SemaphoreType.DMA

    def share_scratch(sent_rows):
        rims = pltpu.VMEM((4, rim * sent_rows, parts), f32)
        tiles = pltpu.VMEM((2 * UNROLL, parts, parts), bf16)
        tmp = pltpu.VMEM((max(blocks, 2 * rim) * PITCH, parts), f32)
        return [
            pltpu.VMEM((blocks, STATE, parts), f32), rims, rims,
            pltpu.VMEM((blocks + 1, 2 * ROWS, parts), bf16),
            pltpu.VMEM((blocks + 1, parts, FEATURES), bf16),
            tiles, tiles, tmp, tmp, tmp, dma((4,)), dma((4,)),
        ]

    acc = pltpu.VMEM(((blocks + 1) * ACC_PITCH, parts), f32)
    tile_scratch = [
        acc, acc,
        pltpu.VMEM((8 * FACE_UNROLL, parts, parts), bf16),
        pltpu.VMEM((blocks + 8, parts), f32),
    ]
    params = pltpu.CompilerParams(vmem_limit_bytes=24 << 20)

    state, *rest = pl.pallas_call(
        begin_kernel,
        out_shape=(state_shape,) + ready + (kept_shape, behind_shape, behind_shape)
        + tuple(like(a) for a in (stress, plastic, cohesion, lists, links, pairs, contact)),
        in_specs=[smem] + [hbm] * 12,
        out_specs=(vmem,) * 15,
        scratch_shapes=[pltpu.SMEM(a.shape, i32) for a in (counts, lists, links, pairs)]
        + [pltpu.VMEM((blocks, parts), f32)]
        + [pltpu.VMEM(a.shape, f32) for a in (position, velocity, mass, density)]
        + [pltpu.VMEM((2, 8, parts), i32)]
        + [dma((15,)), dma((2,)), dma((2,))]
        + share_scratch(LIVE_ROWS),
        compiler_params=pltpu.CompilerParams(
            vmem_limit_bytes=24 << 20, collective_id=0, has_side_effects=True
        ),
        name="begin",
    )(pair_count, *(
        pltpu.with_memory_space_constraint(a, pltpu.MemorySpace.HBM)
        for a in (counts, lists, links, pairs, contact, position, velocity, stress, mass, density, plastic, cohesion)
    ))
    prepared, far_kept, rest = rest[:4], rest[4], rest[5:]
    behind, (stress_v, plastic_v, cohesion_v, lists_v, links_v, pairs_v, contact_v) = rest[:2], rest[2:]
    ints = (pairs_v, pair_count, lists_v, links_v, *behind, contact_v)
    cost = pl.CostEstimate(flops=pairs.shape[1] * parts * parts * 1000, bytes_accessed=8 << 20, transcendentals=0)
    half = pl.pallas_call(
        half_kernel,
        out_shape=state_shape,
        in_specs=[smem] * 7 + [vmem] * 8,
        out_specs=vmem,
        scratch_shapes=tile_scratch,
        compiler_params=params,
        cost_estimate=cost,
        name="half_step",
    )(*ints, *prepared, state, stress_v, plastic_v, cohesion_v)
    prepared = pl.pallas_call(
        again_kernel,
        out_shape=ready,
        in_specs=[smem] * 3 + [vmem] * 2,
        out_specs=(vmem,) * 4,
        scratch_shapes=share_scratch(MOVING_ROWS),
        compiler_params=pltpu.CompilerParams(
            vmem_limit_bytes=24 << 20, collective_id=1, has_side_effects=True
        ),
        name="again",
    )(pair_count, lists_v, pairs_v, half, far_kept)
    outs = pl.pallas_call(
        end_kernel,
        out_shape=(
            shape(position.shape, f32), shape(velocity.shape, f32), shape(stress.shape, f32), shape(plastic.shape, f32)
        ),
        in_specs=[smem] * 7 + [vmem] * 9,
        out_specs=(vmem,) * 4,
        scratch_shapes=tile_scratch,
        compiler_params=params,
        cost_estimate=cost,
        name="full_step",
    )(*ints, *prepared, half, stress_v, plastic_v, cohesion_v, state)
    return tuple(out[None, None] for out in outs)


def solution(mesh):
    def spec(rank):
        return P("strip", "depth", *([None] * (rank - 2)))

    return jax.shard_map(
        shards,
        mesh=mesh,
        in_specs=tuple(spec(r) for r in (5, 5, 5, 4, 4, 4, 4, 3, 4, 2, 4, 5, 3)),
        out_specs=tuple(spec(r) for r in (5, 5, 5, 4)),
        check_vma=False,
    )
```

```python
import jax
import jax.numpy as jnp
from jax import lax
from jax.experimental import pallas as pl
from jax.experimental.pallas import tpu as pltpu
from jax.sharding import PartitionSpec as P

RETURN_ITERS = 4

smooth_len = 1.5
kernel_coef = -105.0 / (3.141592653589793 * 1.5**5)
time_step = 0.25
gravity = 1.0
spin_rate = 2.0
blade_stiff = 4.0
bulk_mod = 2.0
shear_mod = 1.5
friction = 0.25
harden_scale = 0.05
harden_mod = 0.5
relax_rate = 0.7
tau_floor = 0.5
voigt_index = ((0, 3, 5), (3, 1, 4), (5, 4, 2))
voigt_pairs = ((0, 0), (1, 1), (2, 2), (0, 1), (1, 2), (0, 2))

STATE = 16
SOURCES = 26
ROWS = 32
FEATURES = 32
DISTANCES = 24
UNROLL = 32
FACE_UNROLL = 6
PITCH = 36
LIVE_ROWS = 14
MOVING_ROWS = 9
ACC_PITCH = 40
MESH = pl.DeviceIdType.MESH
f32 = jnp.float32
bf16 = jnp.bfloat16


def source_rows(x, v, s, mass, volume):
    rows = [mass]
    rows += [mass * x[k] for k in range(3)]
    rows += [mass * s[c] for c in range(6)]
    for k in range(3):
        i = voigt_index[k]
        rows.append(mass * (s[i[0]] * x[0] + s[i[1]] * x[1] + s[i[2]] * x[2]))
    rows.append(volume)
    rows += [volume * v[k] for k in range(3)]
    rows += [volume * x[k] for k in range(3)]
    for a, b in voigt_pairs:
        rows.append(volume * (0.5 * (v[a] * x[b] + v[b] * x[a])))
    return rows


def split3(value):
    high = value.astype(bf16).astype(f32)
    rest = value - high
    mid = rest.astype(bf16).astype(f32)
    low = (rest - mid).astype(bf16).astype(f32)
    return high, mid, low


PRODUCTS = ((0, 0), (0, 1), (1, 0), (1, 1), (0, 2), (2, 0))


def distance_rows(x, row_side, col_side):
    scaled = [x[k] * (1.0 / smooth_len) for k in range(3)]
    parts = [split3(y) for y in scaled]
    norm = split3(scaled[0] * scaled[0] + scaled[1] * scaled[1] + scaled[2] * scaled[2])
    one = jnp.ones_like(x[0])
    left, right = [], []
    for k in range(3):
        for a, b in PRODUCTS:
            left.append(-2.0 * parts[k][a])
            right.append(parts[k][b])
    left += list(norm) + [one] * 3
    right += [one] * 3 + list(norm)
    return (left if row_side else None, right if col_side else None)


def put_rows(ref, rows, start, count, stride):
    for k, row in enumerate(rows):
        ref[pl.ds(start * stride + k, count, stride=stride), :] = row


def get_row(ref, k, count, stride):
    return ref[pl.ds(k, count, stride=stride), :]


def close_kernel(left, right):
    squared = lax.dot_general(left, right, (((1,), (0,)), ((), ())), preferred_element_type=f32)
    squared = jnp.maximum(squared, 1e-30)
    near = jnp.maximum(1.0 - squared * lax.rsqrt(squared), 0.0)
    return (near * near * near).astype(bf16)


def spread(sources, kernel):
    both = jnp.concatenate([sources[:ROWS], sources[ROWS:]], axis=1)
    twice = jnp.concatenate([kernel, kernel], axis=0)
    return lax.dot_general(both, twice, (((1,), (0,)), ((), ())), preferred_element_type=f32)


def pipelined(steps, width, prepare, apply, finish, beside=None, late=(None, None)):
    for u in range(width):
        prepare(0, u, 0)

    def one(g, half, more):
        found = []
        for u in range(width):
            found += apply(g, u, half)
            if more:
                prepare(g + 1, u, 1 - half)
            if beside is not None:
                beside(g, u)
        finish(g, found)

    def step(i, carry):
        one(2 * i, 0, True)
        one(2 * i + 1, 1, True)
        return carry

    lax.fori_loop(0, steps - 1, step, 0)
    for half in range(2):
        if late[half] is not None:
            late[half]()
        one(2 * steps - 2 + half, half, half == 0)


def split_sources(tmp, b):
    rows = tmp[pl.ds(b * PITCH, ROWS), :]
    high = rows.astype(bf16)
    return high, (rows - high.astype(f32)).astype(bf16)


def store_features(tmps, src, right, left, start, count):
    def one(b, carry):
        high, low = split_sources(tmps[0], b)
        src[start + b, 0:ROWS, :] = high
        src[start + b, ROWS : 2 * ROWS, :] = low
        left[start + b] = tmps[1][pl.ds(b * PITCH, FEATURES), :].T.astype(bf16)
        if right is not None:
            right[start + b] = tmps[2][pl.ds(b * PITCH, FEATURES), :].astype(bf16)
        return carry

    if right is None:
        for b in range(count):
            one(b, 0)
    else:
        lax.fori_loop(0, count, one, 0, unroll=16)


def gather_rims(rows, raw, lists, sends, after):
    for k, row in enumerate(rows):
        raw[:, k, :] = row
    width = len(rows)
    for face in range(4):
        for slot in range(lists.shape[1]):
            sends[face, slot * width : (slot + 1) * width, :] = raw[lists[face, slot]][:width]
        after(face)


class Faces:
    def __init__(self):
        d, n = lax.axis_index("depth"), lax.axis_size("depth")
        s, m = lax.axis_index("strip"), lax.axis_size("strip")
        self.there = (d < n - 1, d > 0, None, None)
        self.device = (
            {"depth": d + 1}, {"depth": d - 1},
            {"strip": lax.rem(s + 1, m)}, {"strip": lax.rem(s + m - 1, m)},
        )

    def when(self, face, act):
        if self.there[face] is None:
            act()
        else:
            pl.when(self.there[face])(act)

    def greet(self):
        barrier = pltpu.get_barrier_semaphore()
        for face in range(4):
            def act(face=face):
                pl.semaphore_signal(barrier, inc=1, device_id=self.device[face], device_id_type=MESH)
            self.when(face, act)

    def meet(self):
        peers = sum(1 if there is None else there.astype(jnp.int32) for there in self.there)
        pl.semaphore_wait(pltpu.get_barrier_semaphore(), peers)

    def copy(self, face, source, target, sent, got):
        return pltpu.make_async_remote_copy(
            src_ref=source, dst_ref=target, send_sem=sent, recv_sem=got,
            device_id=self.device[face], device_id_type=MESH,
        )


def prepare_local(rows, src, right, left, tmps, blocks):
    slots = tmps[0].shape[0] // PITCH
    zero = jnp.zeros((slots, rows[0].shape[1]), f32)
    for tmp, used in zip(tmps, (SOURCES, DISTANCES, DISTANCES)):
        for k in range(used, ROWS):
            tmp[pl.ds(k, slots, stride=PITCH), :] = zero
    sources = source_rows(rows[0:3], rows[3:6], rows[6:12], rows[12], rows[13])
    put_rows(tmps[0], sources, 0, blocks, PITCH)
    left_rows, right_rows = distance_rows(rows[0:3], True, True)
    put_rows(tmps[1], left_rows, 0, blocks, PITCH)
    put_rows(tmps[2], right_rows, 0, blocks, PITCH)
    store_features(tmps, src, right, left, 0, blocks)
    src[blocks] = jnp.zeros(src.shape[1:], bf16)
    right[blocks] = jnp.zeros(right.shape[1:], bf16)
    left[blocks] = jnp.zeros(left.shape[1:], bf16)


def prepare_far(got, start, src, left, tmps):
    count = got[0].shape[0]
    put_rows(tmps[0], source_rows(got[0:3], got[3:6], got[6:12], got[12], got[13]), 0, count, PITCH)
    put_rows(tmps[1], distance_rows(got[0:3], True, False)[0], 0, count, PITCH)
    store_features(tmps, src, None, left, start, count)


def pair_at(pairs, live, q, blocks):
    at = jnp.minimum(q, pairs.shape[1] - 1)
    a, b = pairs[0, at], pairs[1, at]
    return jnp.where(q < live, a, blocks), jnp.where(q < live, b, blocks)


def local_terms(pairs, total, src, right, left, terms, held, turned, late):
    blocks = src.shape[0] - 1
    live = total[0, 0]

    def prepare(g, u, slot):
        a, b = pair_at(pairs, live, g * UNROLL + u, blocks)
        kernel = close_kernel(left[a], right[b])
        held[slot * UNROLL + u] = kernel
        turned[slot * UNROLL + u] = kernel.T

    def apply(g, u, slot):
        q = g * UNROLL + u
        a, b = pair_at(pairs, live, q, blocks)
        at = slot * UNROLL + u
        return [(q, 0, spread(src[b], turned[at])), (q, 1, spread(src[a], held[at]))]

    def finish(g, found):
        for q, side, value in found:
            terms[q, side] = value

    pipelined(terms.shape[0] // (2 * UNROLL), UNROLL, prepare, apply, finish, late=late)


def share(
    faces, rows, first, far_kept, lists, pairs, total, raw, sends, far, sent, got,
    right, far_src, far_left, terms, src, left, held, turned, tmps, extra,
):
    blocks, rim = rows[0].shape[0], lists.shape[1]
    sent_rows = LIVE_ROWS if first else MOVING_ROWS
    copies = [
        faces.copy(face, sends.at[face], far.at[face ^ 1], sent.at[face], got.at[face ^ 1])
        for face in range(4)
    ]

    def after(face):
        if face == 0:
            faces.meet()
        faces.when(face, copies[face].start)

    gather_rims(rows[:LIVE_ROWS] if first else rows[3:12], raw, lists, sends, after)
    extra()
    prepare_local(rows, src, right, left, tmps, blocks)
    far_src[4 * rim] = jnp.zeros(far_src.shape[1:], bf16)
    far_left[4 * rim] = jnp.zeros(far_left.shape[1:], bf16)

    def arrivals(pair):
        for face in pair:
            if faces.there[face] is not None:
                @pl.when(jnp.logical_not(faces.there[face]))
                def _():
                    far[face] = jnp.zeros(far.shape[1:], f32)
            faces.when(face, copies[face ^ 1].wait_recv)
        halves = [[get_row(far.at[face], k, rim, sent_rows) for k in range(sent_rows)] for face in pair]
        arrived = [jnp.concatenate(rows, axis=0) for rows in zip(*halves)]
        kept = slice(pair[0] * rim, (pair[0] + 2) * rim)
        if first:
            far_kept[0, kept], far_kept[1, kept] = arrived[12], arrived[13]
            for k in range(3):
                far_kept[2 + k, kept] = arrived[k] + 0.5 * time_step * arrived[3 + k]
        else:
            arrived = [far_kept[2 + k, kept] for k in range(3)] + arrived
            arrived += [far_kept[0, kept], far_kept[1, kept]]
        prepare_far(arrived, pair[0] * rim, far_src, far_left, tmps)

    strip, depth = (lambda: arrivals((2, 3))), (lambda: arrivals((0, 1)))
    late = (None, strip)
    local_terms(pairs, total, src, right, left, terms, held, turned, late)
    depth()
    for face in range(4):
        faces.when(face, copies[face].wait_send)


def begin_kernel(
    total, counts_in, lists_in, links_in, pairs_in, contact_in, pos_in, vel_in, stress_in, mass_in, density_in,
    plastic_in, cohesion_in,
    state, right, far_src, far_left, terms, far_kept, behind_depth, behind_strip,
    stress, plastic, cohesion, lists_out, links_out, pairs_out, contact,
    counts, lists, links, pairs, occ, pos, vel, mass, density, packed,
    sems, pack_sent, pack_got,
    raw, sends, far, src, left, held, turned, tmp0, tmp1, tmp2, sent, got,
):
    faces = Faces()
    faces.greet()
    moved = (
        (counts_in, counts), (lists_in, lists), (pos_in, pos), (vel_in, vel), (stress_in, stress),
        (mass_in, mass), (density_in, density), (links_in, links),
        (plastic_in, plastic), (cohesion_in, cohesion),
        (lists_in, lists_out), (links_in, links_out), (pairs_in, pairs_out), (contact_in, contact),
        (pairs_in, pairs),
    )
    copies = [pltpu.make_async_copy(a, b, sems.at[i]) for i, (a, b) in enumerate(moved)]
    for copy in copies:
        copy.start()
    blocks, parts = mass.shape
    lane = lax.broadcasted_iota(jnp.int32, (1, parts), 1)
    packed[...] = jnp.zeros(packed.shape, jnp.int32)
    copies[0].wait()
    for b in range(blocks):
        occ[b : b + 1, :] = jnp.where(lane < counts[0, b], 1.0, 0.0)
    live = occ[...]
    for copy in copies[1:7] + copies[14:]:
        copy.wait()
    rho = density[...]
    inverse = 1.0 / (rho * rho)
    weighted = mass[...] * live * kernel_coef
    rows = [pos[k] for k in range(3)] + [vel[k] for k in range(3)]
    rows += [stress[c] * inverse for c in range(6)]
    rows += [weighted, weighted / rho, live, inverse]
    for k, row in enumerate(rows):
        state[k] = row
    packs = (
        faces.copy(0, packed.at[0], behind_depth, pack_sent.at[0], pack_got.at[0]),
        faces.copy(2, packed.at[1], behind_strip, pack_sent.at[1], pack_got.at[1]),
    )

    def extra():
        copies[7].wait()
        for face in range(2):
            for side in range(2):
                row = jnp.zeros((1, parts), jnp.int32)
                for q in range(links.shape[2]):
                    row = jnp.where(lane == q, links[face, side, q], row)
                packed[face, side : side + 1, :] = row
            faces.when(2 * face, packs[face].start)

    share(
        faces, rows, True, far_kept, lists, pairs, total, raw, sends, far, sent, got,
        right, far_src, far_left, terms, src, left, held, turned, (tmp0, tmp1, tmp2), extra,
    )

    @pl.when(jnp.logical_not(faces.there[1]))
    def _():
        behind_depth[...] = jnp.zeros(behind_depth.shape, jnp.int32)

    faces.when(1, packs[0].wait_recv)
    packs[1].wait_recv()
    faces.when(0, packs[0].wait_send)
    packs[1].wait_send()
    for copy in copies[8:14]:
        copy.wait()


def again_kernel(
    total, lists, pairs, state, far_kept, right, far_src, far_left, terms,
    raw, sends, far, src, left, held, turned, tmp0, tmp1, tmp2, sent, got,
):
    faces = Faces()
    faces.greet()
    rows = [state[k] for k in range(STATE)]
    share(
        faces, rows, False, far_kept, lists, pairs, total, raw, sends, far, sent, got,
        right, far_src, far_left, terms, src, left, held, turned, (tmp0, tmp1, tmp2),
        lambda: None,
    )


def add_block(acc, at, value):
    rows = pl.ds(pl.multiple_of(at * ACC_PITCH, 8), ROWS)
    acc[rows, :] += value


def sums(pairs, total, lists, links, links_behind, right, src, left, terms, acc, own_acc, held):
    acc[...] = jnp.zeros(acc.shape, f32)
    own_acc[...] = jnp.zeros(own_acc.shape, f32)
    rim = lists.shape[1]
    blocks = right.shape[0] - 1
    live = total[0, 0]
    cross = links.shape[2]
    whole = cross % (2 * FACE_UNROLL) == 0

    def entry(g, u):
        q = g * FACE_UNROLL + u // 4
        at = jnp.minimum(q, cross - 1)
        face, behind = (u % 4) // 2, u % 2
        if behind:
            own = lists[2 * face + 1, links_behind[face][1, at]]
            far_slot = links_behind[face][0, at]
        else:
            own, far_slot = lists[2 * face, links[face, 0, at]], links[face, 1, at]
        far_slot = (u % 4) * rim + far_slot
        return own, far_slot if whole else jnp.where(q < cross, far_slot, 4 * rim)

    width = 4 * FACE_UNROLL

    def prepare(g, u, slot):
        own, far_slot = entry(g, u)
        held[slot * width + u] = close_kernel(left[far_slot], right[own])

    def apply(g, u, slot):
        own, far_slot = entry(g, u)
        return [(own, spread(src[far_slot], held[slot * width + u]))]

    steps = (cross + 2 * FACE_UNROLL - 1) // (2 * FACE_UNROLL)
    count = pairs.shape[1]
    share_of = (count + 2 * steps - 1) // (2 * steps)
    assert share_of <= width

    def beside(g, u):
        if u < share_of:
            q = g * share_of + u
            a, b = pair_at(pairs, live, q, blocks)
            at = jnp.minimum(q, count - 1)
            add_block(own_acc, a, terms[at, 0])
            add_block(own_acc, jnp.where(a == b, blocks, b), terms[at, 1])

    def finish(g, found):
        for at, value in found:
            add_block(acc, at, value)

    pipelined(steps, width, prepare, apply, finish, beside)


def section_rates(summed, x, v, s, contact_flag):
    blade = (spin_rate * x[2], jnp.zeros_like(x[1]), -spin_rate * x[0])
    acceleration = []
    arm = [x[l] * summed[0] - summed[1 + l] for l in range(3)]
    for k in range(3):
        total = -summed[10 + k] + blade_stiff * contact_flag * (blade[k] - v[k])
        for l in range(3):
            slot = voigt_index[k][l]
            total = total + s[slot] * arm[l] + x[l] * summed[4 + slot]
        if k == 2:
            total = total - gravity
        acceleration.append(total)
    strain = []
    for c, (k, l) in enumerate(voigt_pairs):
        rate = 0.5 * (x[l] * summed[14 + k] + x[k] * summed[14 + l]) - summed[20 + c]
        rate = rate - 0.5 * summed[13] * (v[k] * x[l] + v[l] * x[k])
        rate = rate + 0.5 * (v[k] * summed[17 + l] + v[l] * summed[17 + k])
        strain.append(rate)
    return acceleration, strain


def elastic_step(stress, strain, fraction):
    volumetric = strain[0] + strain[1] + strain[2]
    lame_first = bulk_mod - 2.0 * shear_mod / 3.0
    components = []
    for c in range(6):
        change = 2.0 * shear_mod * strain[c]
        if c < 3:
            change = change + lame_first * volumetric
        components.append(stress[c] + fraction * time_step * change)
    return components


def plastic_return(c, plastic, cohesion):
    for _ in range(RETURN_ITERS):
        mean = (c[0] + c[1] + c[2]) / 3.0
        d = [c[0] - mean, c[1] - mean, c[2] - mean, c[3], c[4], c[5]]
        second = 0.5 * (d[0] * d[0] + d[1] * d[1] + d[2] * d[2])
        second = second + d[3] * d[3] + d[4] * d[4] + d[5] * d[5]
        tau = jnp.sqrt(second)
        limit = cohesion * (1.0 + plastic / (plastic + harden_scale))
        excess = jnp.maximum(tau + friction * 3.0 * mean - limit, 0.0)
        multiplier = (
            relax_rate * excess / (shear_mod + 9.0 * bulk_mod * friction * friction + harden_mod)
        )
        shrink = jnp.maximum(1.0 - shear_mod * multiplier / jnp.maximum(tau, tau_floor), 0.0)
        mean = mean - 3.0 * bulk_mod * friction * multiplier
        c = [
            d[0] * shrink + mean,
            d[1] * shrink + mean,
            d[2] * shrink + mean,
            d[3] * shrink,
            d[4] * shrink,
            d[5] * shrink,
        ]
        plastic = plastic + multiplier
    return c, plastic


def contact_rows(contact, flag, blocks):
    flag[...] = jnp.zeros_like(flag)
    for i in range(contact.shape[1]):
        flag[pl.ds(contact[0, i], 1), :] += 1.0
    return flag[0:blocks, :]


def rates_of(acc, own_acc, state, contact, flag):
    blocks, parts = state.shape[1:]
    contact_flag = contact_rows(contact, flag, blocks)
    x = [state[k] for k in range(3)]
    v = [state[k] for k in range(3, 6)]
    s = [state[k] for k in range(6, 12)]
    summed = [get_row(acc, k, blocks, ACC_PITCH) + get_row(own_acc, k, blocks, ACC_PITCH) for k in range(SOURCES)]
    return x, v, *section_rates(summed, x, v, s, contact_flag)


def half_kernel(
    pairs, total, lists, links, behind_depth, behind_strip, contact,
    right, far_src, far_left, terms, state, stress, plastic, cohesion,
    state_out,
    acc, own_acc, held, flag,
):
    sums(
        pairs, total, lists, links, (behind_depth, behind_strip),
        right, far_src, far_left, terms, acc, own_acc, held,
    )
    x, v, acceleration, strain = rates_of(acc, own_acc, state, contact, flag)
    components, _ = plastic_return(
        elastic_step([stress[c] for c in range(6)], strain, 0.5), plastic[...], cohesion[...]
    )
    inverse = state[15]
    rows = [x[k] + 0.5 * time_step * v[k] for k in range(3)]
    rows += [v[k] + 0.5 * time_step * acceleration[k] for k in range(3)]
    rows += [c * inverse for c in components]
    rows += [state[12], state[13], state[14], inverse]
    for k, row in enumerate(rows):
        state_out[k] = row


def end_kernel(
    pairs, total, lists, links, behind_depth, behind_strip, contact,
    right, far_src, far_left, terms, state, stress, plastic, cohesion, first,
    new_position, new_velocity, new_stress, new_plastic,
    acc, own_acc, held, flag,
):
    sums(
        pairs, total, lists, links, (behind_depth, behind_strip),
        right, far_src, far_left, terms, acc, own_acc, held,
    )
    _, half_v, acceleration, strain = rates_of(acc, own_acc, state, contact, flag)
    components, hardened = plastic_return(
        elastic_step([stress[c] for c in range(6)], strain, 1.0), plastic[...], cohesion[...]
    )
    live = state[14]
    for k in range(3):
        new_position[k] = (first[k] + time_step * half_v[k]) * live
        new_velocity[k] = (first[3 + k] + time_step * acceleration[k]) * live
    for c in range(6):
        new_stress[c] = components[c] * live
    new_plastic[...] = hardened * live


def shards(
    position, velocity, stress, plastic, particle_mass, density, cohesion,
    counts, block_pairs, pair_count, send_lists, cross_links, contact,
):
    position, velocity, stress = position[0, 0], velocity[0, 0], stress[0, 0]
    plastic, mass, density, cohesion = plastic[0, 0], particle_mass[0, 0], density[0, 0], cohesion[0, 0]
    counts, pairs, lists = counts[0], jnp.swapaxes(block_pairs[0, 0], 0, 1), send_lists[0, 0]
    links, contact = jnp.swapaxes(cross_links[0, 0], 1, 2), contact[0]
    blocks, parts = mass.shape
    rim = lists.shape[1]
    smem = pl.BlockSpec(memory_space=pltpu.SMEM)
    vmem = pl.BlockSpec(memory_space=pltpu.VMEM)
    hbm = pl.BlockSpec(memory_space=pltpu.MemorySpace.HBM)
    shape = jax.ShapeDtypeStruct
    i32 = jnp.int32

    def like(a):
        return shape(a.shape, a.dtype)

    state_shape = shape((STATE, blocks, parts), f32)
    count = pairs.shape[1]
    slots = (count + 2 * UNROLL - 1) // (2 * UNROLL) * (2 * UNROLL)
    ready = (
        shape((blocks + 1, FEATURES, parts), bf16),
        shape((4 * rim + 1, 2 * ROWS, parts), bf16),
        shape((4 * rim + 1, parts, FEATURES), bf16),
        shape((slots, 2, ROWS, parts), f32),
    )
    kept_shape = shape((5, 4 * rim, parts), f32)
    behind_shape = shape((8, parts), i32)
    dma = pltpu.SemaphoreType.DMA

    def share_scratch(sent_rows):
        rims = pltpu.VMEM((4, rim * sent_rows, parts), f32)
        tiles = pltpu.VMEM((2 * UNROLL, parts, parts), bf16)
        tmp = pltpu.VMEM((max(blocks, 2 * rim) * PITCH, parts), f32)
        return [
            pltpu.VMEM((blocks, STATE, parts), f32), rims, rims,
            pltpu.VMEM((blocks + 1, 2 * ROWS, parts), bf16),
            pltpu.VMEM((blocks + 1, parts, FEATURES), bf16),
            tiles, tiles, tmp, tmp, tmp, dma((4,)), dma((4,)),
        ]

    acc = pltpu.VMEM(((blocks + 1) * ACC_PITCH, parts), f32)
    tile_scratch = [
        acc, acc,
        pltpu.VMEM((8 * FACE_UNROLL, parts, parts), bf16),
        pltpu.VMEM((blocks + 8, parts), f32),
    ]
    params = pltpu.CompilerParams(vmem_limit_bytes=24 << 20)

    state, *rest = pl.pallas_call(
        begin_kernel,
        out_shape=(state_shape,) + ready + (kept_shape, behind_shape, behind_shape)
        + tuple(like(a) for a in (stress, plastic, cohesion, lists, links, pairs, contact)),
        in_specs=[smem] + [hbm] * 12,
        out_specs=(vmem,) * 15,
        scratch_shapes=[pltpu.SMEM(a.shape, i32) for a in (counts, lists, links, pairs)]
        + [pltpu.VMEM((blocks, parts), f32)]
        + [pltpu.VMEM(a.shape, f32) for a in (position, velocity, mass, density)]
        + [pltpu.VMEM((2, 8, parts), i32)]
        + [dma((15,)), dma((2,)), dma((2,))]
        + share_scratch(LIVE_ROWS),
        compiler_params=pltpu.CompilerParams(
            vmem_limit_bytes=24 << 20, collective_id=0, has_side_effects=True
        ),
        name="begin",
    )(pair_count, *(
        pltpu.with_memory_space_constraint(a, pltpu.MemorySpace.HBM)
        for a in (counts, lists, links, pairs, contact, position, velocity, stress, mass, density, plastic, cohesion)
    ))
    prepared, far_kept, rest = rest[:4], rest[4], rest[5:]
    behind, (stress_v, plastic_v, cohesion_v, lists_v, links_v, pairs_v, contact_v) = rest[:2], rest[2:]
    ints = (pairs_v, pair_count, lists_v, links_v, *behind, contact_v)
    cost = pl.CostEstimate(flops=pairs.shape[1] * parts * parts * 1000, bytes_accessed=8 << 20, transcendentals=0)
    half = pl.pallas_call(
        half_kernel,
        out_shape=state_shape,
        in_specs=[smem] * 7 + [vmem] * 8,
        out_specs=vmem,
        scratch_shapes=tile_scratch,
        compiler_params=params,
        cost_estimate=cost,
        name="half_step",
    )(*ints, *prepared, state, stress_v, plastic_v, cohesion_v)
    prepared = pl.pallas_call(
        again_kernel,
        out_shape=ready,
        in_specs=[smem] * 3 + [vmem] * 2,
        out_specs=(vmem,) * 4,
        scratch_shapes=share_scratch(MOVING_ROWS),
        compiler_params=pltpu.CompilerParams(
            vmem_limit_bytes=24 << 20, collective_id=1, has_side_effects=True
        ),
        name="again",
    )(pair_count, lists_v, pairs_v, half, far_kept)
    outs = pl.pallas_call(
        end_kernel,
        out_shape=(
            shape(position.shape, f32), shape(velocity.shape, f32), shape(stress.shape, f32), shape(plastic.shape, f32)
        ),
        in_specs=[smem] * 7 + [vmem] * 9,
        out_specs=(vmem,) * 4,
        scratch_shapes=tile_scratch,
        compiler_params=params,
        cost_estimate=cost,
        name="full_step",
    )(*ints, *prepared, half, stress_v, plastic_v, cohesion_v, state)
    return tuple(out[None, None] for out in outs)


def solution(mesh):
    def spec(rank):
        return P("strip", "depth", *([None] * (rank - 2)))

    return jax.shard_map(
        shards,
        mesh=mesh,
        in_specs=tuple(spec(r) for r in (5, 5, 5, 4, 4, 4, 4, 3, 4, 2, 4, 5, 3)),
        out_specs=tuple(spec(r) for r in (5, 5, 5, 4)),
        check_vma=False,
    )
```
